32 devices in a mesh: tile: 8 (over z, x), member: 4 (over y, core).
Axes of the slice: x: 2, y: 2, z: 4, core: 2. Of those that a mesh axis runs over, the one named last changes fastest.
Arguments:
- noise: float32 [4, 512, 512], P('member', 'tile'), as said below
- observed: bfloat16 [2, 6, 512, 512], P(None, None, 'tile'), may hold values from -6 to 6
- row_shift: int32 [512, 512], P('tile'), may hold values from -4 to 4
- col_shift: int32 [512, 512], P('tile'), may hold values from -4 to 4
- rain_mask: int32 [64, 4], P('tile'), may hold values 0 or 1
- autocorr: float32 [2, 6], replicated, may hold values from 0.09 to 0.97, as said below
- level_scale: float32 [6], replicated, may hold values from 0.2 to 2
Outputs:
- forecast: bfloat16 [4, 512, 512], P('member', 'tile')
- ensemble_mean: float32 [512, 512], P('tile')
The draws below stay inside these ranges and needn't reach their ends.
Inputs may be any that keep to these rules, and one draw needn't show every extreme that they name: row_shift, along with col_shift, is bounded by 4 in magnitude. `autocorr`: row 1 of each level lies between the square of row 0 and row 0. `noise`: finite values.
All inputs are finite; a program needn't handle non-finite values. No bound on the sum of `rain_mask` on one device may be relied on, other than what follows from the above.
Results may differ from the reference program's by a relative error of at most 0.01.
Values may be sent and summed in bfloat16 or wider, within the bound.
A program may use at most 64 MiB of HBM per device.

```python
import math
import jax
import jax.numpy as jnp
from jax import lax

NY = 512
NX = 512
LEVELS = 6
HALO = 4
MEMBERS = 4


def draw_noise(key, part):
    first, second, third = jax.random.split(key, 3)
    rise = jnp.exp(math.log(3.0) * jnp.arange(NY).astype(jnp.float32) / NY)
    base = jax.random.normal(first, (MEMBERS, NY, NX), jnp.float32)
    row_scale = rise * jnp.exp(jax.random.uniform(second, (NY,), jnp.float32, 0.0, math.log(4.0)))
    col_scale = jnp.exp(jax.random.uniform(third, (NX,), jnp.float32, 0.0, math.log(10.0)))
    return base * row_scale[None, :, None] * col_scale[None, None, :]


def draw_autocorr(key, part):
    first, second = jax.random.split(jax.random.fold_in(key, 7))
    lag_one = jax.random.uniform(first, (LEVELS,), jnp.float32, 0.3, 0.97)
    fraction = jax.random.uniform(second, (LEVELS,), jnp.float32, 0.0, 0.9)
    lag_two = lag_one * lag_one + fraction * (lag_one - lag_one * lag_one)
    return jnp.stack([lag_one, lag_two])


def touch_ends(result, key, least, top_value):
    longest = result.shape.index(max(result.shape))
    spots = []
    for shift in (0, 1):
        where = [jax.random.randint(jax.random.fold_in(key, axis), (), 0, length) for axis, length in enumerate(result.shape)]
        where[longest] = (where[longest] + shift) % result.shape[longest]
        spots.append(tuple(where))
    return result.at[spots[0]].set(least).at[spots[1]].set(top_value)


def level_of(own_key, shape, pieces, least, largest):
    level = 1.0
    for position, blocks in pieces:
        draws = jax.random.uniform(jax.random.fold_in(jax.random.fold_in(own_key, 6), position), (blocks,), jnp.float32, least / len(pieces), largest / len(pieces))
        level = level * jnp.repeat(jnp.exp(draws), shape[position] // blocks).reshape((-1,) + (1,) * (len(shape) - 1 - position))
    return level


def bell_draw(key, extent, width, limit, cuts=(), held_as=jnp.bfloat16):
    drawn = jax.random.normal(key, extent, jnp.float32) * width
    if len(cuts) > 0:
        drawn = level_of(key, extent, cuts, -0.22, 0.18) * drawn
    return jnp.clip(drawn, min=-limit, max=limit).astype(held_as)


def setup_inputs(seed: int = 0) -> dict:
    arg_keys = jax.random.split(jax.random.key(seed), 8)
    noise = draw_noise(jax.random.fold_in(arg_keys[7], 71), 0)
    observed = bell_draw(arg_keys[1], (2, LEVELS, NY, NX), 1.0, 6.0, ((2, 8),))
    row_shift = touch_ends(jax.random.randint(arg_keys[2], (NY, NX), 0 - HALO, HALO + 1), jax.random.fold_in(arg_keys[2], 1), 0 - HALO, HALO).astype(jnp.int32)
    col_shift = touch_ends(jax.random.randint(arg_keys[3], (NY, NX), 0 - HALO, HALO + 1), jax.random.fold_in(arg_keys[3], 1), 0 - HALO, HALO).astype(jnp.int32)
    rain_mask = touch_ends((jax.random.randint(arg_keys[4], (NY // 8, NX // 128), 0, 4) < 3).astype(jnp.int32), jax.random.fold_in(arg_keys[4], 1), 0, 1)
    autocorr = draw_autocorr(jax.random.fold_in(arg_keys[7], 71), 0)
    level_scale = jnp.clip(jnp.exp(jax.random.uniform(arg_keys[6], (LEVELS,), jnp.float32, math.log(0.2), math.log(2.0))), 0.2, 2.0)
    return dict(noise=noise, observed=observed, row_shift=row_shift, col_shift=col_shift, rain_mask=rain_mask, autocorr=autocorr, level_scale=level_scale)


def band_weights(freq_y, freq_x, levels, longest):
    radius = longest * jnp.sqrt(freq_y[:, None] * freq_y[:, None] + freq_x[None, :] * freq_x[None, :])
    log_radius = jnp.log(radius + 1.0)
    spacing = math.log(longest / 2.0) / (levels - 1)
    centres = spacing * jnp.arange(levels).astype(jnp.float32)
    spread = 0.6 * spacing
    offsets = log_radius[:, None, :] - centres[None, :, None]
    bumps = jnp.exp(-(offsets * offsets) / (2.0 * spread * spread))
    return bumps / lax.optimization_barrier(jnp.sum(bumps, axis=1, keepdims=True))

def advect(observed, row_shift, col_shift):
    padded = jnp.pad(observed, ((0, 0), (0, 0), (HALO, HALO), (HALO, HALO)))
    row_span = NX + 2 * HALO
    flattened = padded.reshape(2, LEVELS, -1)
    rows_at = jnp.arange(NY, dtype=jnp.int32)[:, None] + HALO - row_shift
    cols_at = jnp.arange(NX, dtype=jnp.int32)[None, :] + HALO - col_shift
    source_index = (rows_at * row_span + cols_at).reshape(-1).astype(jnp.int32)
    return jnp.take(flattened, source_index, axis=2).reshape(2, LEVELS, NY, NX)

def reference(noise, observed, row_shift, col_shift, rain_mask, autocorr, level_scale):
    lag_one = autocorr[0]
    lag_two = autocorr[1]
    shared_den = 1.0 - lag_one * lag_one
    phi_one = lag_one * (1.0 - lag_two) / shared_den
    phi_two = (lag_two - lag_one * lag_one) / shared_den
    innovation = jnp.sqrt(1.0 - phi_one * lag_one - phi_two * lag_two)
    moved = advect(observed, row_shift, col_shift).astype(jnp.float32)
    deterministic_share = lax.optimization_barrier(jnp.sum((level_scale * phi_one)[:, None, None] * moved[0] + (level_scale * phi_two)[:, None, None] * moved[1], axis=0))
    wave_y = jnp.arange(NY, dtype=jnp.int32)
    wave_x = jnp.arange(NX, dtype=jnp.int32)
    freq_y = jnp.minimum(wave_y, NY - wave_y).astype(jnp.float32) / NY
    freq_x = jnp.minimum(wave_x, NX - wave_x).astype(jnp.float32) / NX
    weights = jnp.moveaxis(band_weights(freq_y, freq_x, LEVELS, max(NY, NX)), 1, 0)
    precipitation = jnp.repeat(jnp.repeat(rain_mask, 8, axis=0), 128, axis=1).astype(jnp.float32)

    def one_member(member_field):
        spectrum = jnp.fft.fft2(member_field)

        def one_level(band):
            return jnp.real(jnp.fft.ifft2(band * spectrum))
        level_fields = lax.map(one_level, weights)
        level_power = lax.optimization_barrier(jnp.sum(level_fields * level_fields, axis=(1, 2))) / (NY * NX)
        level_coef = level_scale * innovation / jnp.sqrt(level_power + 1e-06)
        return lax.optimization_barrier(jnp.sum(level_coef[:, None, None] * level_fields, axis=0))
    random_perturbation = lax.map(one_member, noise)
    prediction_before_clipping = precipitation[None] * (deterministic_share[None] + random_perturbation)
    return (prediction_before_clipping.astype(jnp.bfloat16), lax.optimization_barrier(jnp.mean(prediction_before_clipping, axis=0)))
```

```python
import functools
import math

import jax
import jax.numpy as jnp
import numpy as np
from jax import lax
from jax.experimental import pallas as pl
from jax.experimental.pallas import tpu as pltpu
from jax.sharding import PartitionSpec as P

LEVELS = 6
HALO = 4
PAD = 8
F32 = jnp.float32
BF16 = jnp.bfloat16


def real_basis(length):
    half = length // 2
    positions = np.arange(length)
    angles = 2.0 * math.pi * (np.outer(np.arange(half), positions) % length) / length
    cosines = np.cos(angles) * math.sqrt(2.0 / length)
    sines = np.sin(angles) * math.sqrt(2.0 / length)
    cosines[0] = 1.0 / math.sqrt(length)
    sines[0] = (1.0 - 2.0 * (positions % 2)) / math.sqrt(length)
    return np.concatenate([cosines, sines], axis=0)


def band_table(height, width):
    freq_y = np.arange(height // 2 + PAD)[:, None] / height
    freq_x = np.arange(width // 2 + 128)[None, :] / width
    longest = max(height, width)
    log_radius = np.log(longest * np.sqrt(freq_y * freq_y + freq_x * freq_x) + 1.0)
    spacing = math.log(longest / 2.0) / (LEVELS - 1)
    offsets = log_radius[None] - spacing * np.arange(LEVELS)[:, None, None]
    bumps = np.exp(-(offsets * offsets) / (2.0 * (0.6 * spacing) ** 2))
    return bumps / np.sum(bumps, axis=0, keepdims=True)


def chunk_of(rows):
    return rows // 2 if rows % 32 == 0 else rows


def split(value):
    high = value.astype(BF16)
    return high, (value - high.astype(F32)).astype(BF16)


def dot(a, b):
    return jnp.dot(a, b, preferred_element_type=F32)


def coefficients(ac, scale, k, width):
    g1 = jnp.full((1, width), ac[0, k], F32)
    g2 = jnp.full((1, width), ac[1, k], F32)
    s = jnp.full((1, width), scale[k], F32)
    den = 1.0 - g1 * g1
    one = g1 * (1.0 - g2) / den
    two = (g2 - g1 * g1) / den
    innovation = jnp.sqrt(1.0 - one * g1 - two * g2)
    return s * one, s * two, s * innovation


def write_out(fc, mean, fc_hbm, mean_hbm, sem):
    copies = [pltpu.make_async_copy(a, b, sem.at[i]) for i, (a, b) in enumerate([(fc, fc_hbm), (mean, mean_hbm)])]
    for copy in copies:
        copy.start()
    for copy in copies:
        copy.wait()


def kernel(
    tiles, pair, members,
    noise_hbm, obs_hbm, row_hbm, col_hbm, rain_hbm, ac_hbm, scale_hbm, ty_hbm, tx_hbm, txt_hbm, tyt_hbm, band_hbm,
    fc_out, mean,
    noise, obs, row, col, ty, tx, txt, txtl, rows_t, band,
    xg, pad, shifted, steady, mask, spec, gain, arrived, rain, ac, scale,
    load_sem, send_sem, cross_sem, recv_sem, halo_send, halo_recv, mem_send, mem_recv,
):
    fc = fc_out.at[0]
    rows, width = noise.shape
    height = rows * tiles
    hy, hx = height // 2, width // 2
    depth = tiles // pair
    size = chunk_of(rows)
    chunks = rows // size
    t = lax.axis_index("tile")
    m = lax.axis_index("member")
    z = t // pair
    x = t % pair

    sources = [
        (noise_hbm.at[0], noise), (txt_hbm.at[0], txt), (txt_hbm.at[1], txtl),
        (rain_hbm, rain), (ac_hbm, ac), (scale_hbm, scale), (obs_hbm, obs), (row_hbm, row), (col_hbm, col),
        (ty_hbm, ty), (band_hbm, band),
        (tyt_hbm.at[:, pl.ds(pl.multiple_of(t * rows, rows), rows), :], rows_t), (tx_hbm, tx),
    ]
    loads = [pltpu.make_async_copy(a, b, load_sem.at[i]) for i, (a, b) in enumerate(sources)]
    for load in loads[:3]:
        load.start()

    barrier = pltpu.get_barrier_semaphore()
    greeted = 0
    near = sorted({pair * d for d in range(1, depth)} | {1})
    for step in [sign * d for d in near for sign in (-1, 1)]:
        there = jnp.logical_and(t + step >= 0, t + step < tiles)
        greeted = greeted + there.astype(jnp.int32)

        @pl.when(there)
        def _():
            pl.semaphore_signal(barrier, inc=1, device_id={"tile": t + step}, device_id_type=pl.DeviceIdType.MESH)

    for d in range(1, members):
        pl.semaphore_signal(
            barrier, inc=1, device_id={"member": (m + d) % members}, device_id_type=pl.DeviceIdType.MESH
        )

    for load in loads[3:]:
        load.start()
    for load in loads[:3]:
        load.wait()
    own = pl.multiple_of(t * rows, rows)
    n_hi, n_lo = split(noise[...])
    first = dot(jnp.concatenate([n_hi, n_lo], axis=0), txt[...])
    xg[pl.ds(own, rows), :] = (first[:rows] + first[rows:] + dot(n_hi, txtl[...])).astype(BF16)
    pl.semaphore_wait(barrier, greeted + members - 1)

    def part(block, c):
        return xg.at[pl.ds(pl.multiple_of(block * rows + c * size, size), size), :]

    def along(up, d, c):
        mine = part(t, c)
        return pltpu.make_async_remote_copy(
            src_ref=mine, dst_ref=mine, send_sem=send_sem.at[up, d, c], recv_sem=recv_sem.at[t, c],
            device_id={"tile": t + pair * (d if up else -d)}, device_id_type=pl.DeviceIdType.MESH,
        )

    def across(zb, c):
        block = part(zb * pair + x, c)
        return pltpu.make_async_remote_copy(
            src_ref=block, dst_ref=block, send_sem=cross_sem.at[zb, c], recv_sem=recv_sem.at[zb * pair + x, c],
            device_id={"tile": z * pair + 1 - x}, device_id_type=pl.DeviceIdType.MESH,
        )

    def arrival(block, c):
        pltpu.make_async_copy(part(block, c), part(block, c), recv_sem.at[block, c]).wait()

    def both_ways(d, act):
        @pl.when(z + d < depth)
        def _():
            act(1)

        @pl.when(z - d >= 0)
        def _():
            act(0)

    for c in range(chunks):
        if pair > 1:
            across(z, c).start()
        for d in range(depth - 1, 0, -1):
            both_ways(d, lambda up: along(up, d, c).start())

    def relay(s):
        def take(up, c):
            zb = z + s if up else z - s
            arrival(zb * pair + x, c)
            if pair > 1:
                across(zb, c).start()

        for c in range(chunks):
            both_ways(s, lambda up: take(up, c))

    for load in loads[3:7]:
        load.wait()
    coef = [coefficients(ac, scale, k, width) for k in range(LEVELS)]
    for g in range(rows // 16):
        span = pl.ds(16 * g, 16)
        total = jnp.zeros((16, width), F32)
        for k in range(LEVELS):
            total += coef[k][0] * obs[0, k, span, :].astype(F32) + coef[k][1] * obs[1, k, span, :].astype(F32)
        pad[pl.ds(PAD + 16 * g, 16), :] = total
    for i in range(rows // 8):
        for j in range(width // 128):
            mask[8 * i : 8 * i + 8, 128 * j : 128 * j + 128] = jnp.full((8, 128), rain[j, i].astype(F32), F32)

    after = pltpu.make_async_remote_copy(
        src_ref=pad.at[pl.ds(rows, PAD), :], dst_ref=pad.at[pl.ds(0, PAD), :],
        send_sem=halo_send.at[0], recv_sem=halo_recv.at[0],
        device_id={"tile": t + 1}, device_id_type=pl.DeviceIdType.MESH,
    )
    before = pltpu.make_async_remote_copy(
        src_ref=pad.at[pl.ds(PAD, PAD), :], dst_ref=pad.at[pl.ds(rows + PAD, PAD), :],
        send_sem=halo_send.at[1], recv_sem=halo_recv.at[1],
        device_id={"tile": t - 1}, device_id_type=pl.DeviceIdType.MESH,
    )

    @pl.when(t < tiles - 1)
    def _():
        after.start()

    @pl.when(t == tiles - 1)
    def _():
        pad[rows + PAD :, :] = jnp.zeros((PAD, width), F32)

    @pl.when(t > 0)
    def _():
        before.start()

    @pl.when(t == 0)
    def _():
        pad[:PAD, :] = jnp.zeros((PAD, width), F32)

    def shift_columns():
        lane = lax.broadcasted_iota(jnp.int32, (rows + 2 * PAD, width), 1)
        value = pad[...]
        for dx in range(-HALO, HALO + 1):
            moved = pltpu.roll(value, dx % width, 1) if dx else value
            if dx > 0:
                moved = jnp.where(lane >= dx, moved, 0.0)
            if dx < 0:
                moved = jnp.where(lane < width + dx, moved, 0.0)
            shifted[dx + HALO] = moved

    def gather_rows(start, stop):
        for g in range(start, stop):
            span = pl.ds(8 * g, 8)
            code = row[span, :] * (2 * HALO + 1) + col[span, :]
            total = jnp.zeros((8, width), F32)
            for dy in range(-HALO, HALO + 1):
                for dx in range(-HALO, HALO + 1):
                    total = jnp.where(
                        code == dy * (2 * HALO + 1) + dx,
                        shifted[dx + HALO, 8 * g + PAD - dy : 8 * g + PAD - dy + 8, :],
                        total,
                    )
            steady[span, :] = total

    for s in range(1, depth):
        relay(s)

    @pl.when(t > 0)
    def _():
        after.wait_recv()

    @pl.when(t < tiles - 1)
    def _():
        before.wait_recv()

    groups = rows // 8
    shift_columns()
    loads[7].wait()
    loads[8].wait()
    steps = max(depth - 1, 1)
    for s in range(1, depth):
        gather_rows(groups * (s - 1) // steps, groups * s // steps)
    if depth == 1:
        gather_rows(0, groups)
    for load in loads[9:]:
        load.wait()
    if pair > 1:
        for zb in range(depth):
            for c in range(chunks):
                arrival(zb * pair + 1 - x, c)

    spec[...] = dot(ty[...], xg[...])
    strip = 16
    lane = lax.broadcasted_iota(jnp.int32, (strip, hx), 1)
    lane_one = lax.broadcasted_iota(jnp.int32, (strip, 128), 1)
    sub = lax.broadcasted_iota(jnp.int32, (strip, hx), 0)

    def fold(value):
        return value[:8] + value[8:]

    def powers(i, sums):
        r = pl.multiple_of(i * strip, strip)
        top = pl.ds(r, strip)
        low = pl.ds(hy + r, strip)
        cc, cs = spec[top, :hx], spec[top, hx:]
        sc, ss = spec[low, :hx], spec[low, hx:]
        cc, cs, sc, ss = cc * cc, cs * cs, sc * sc, ss * ss
        inner = sub + r > 0
        sc = jnp.where(inner, sc, 0.0)
        ss = jnp.where(inner, ss, 0.0)
        right = cs + ss
        energy = cc + sc + jnp.where(lane > 0, right, 0.0)
        edge = jnp.where(lane_one == 0, right[:, :128], 0.0)
        out = []
        for k in range(LEVELS):
            w = band[k, top, :hx].astype(F32)
            e = band[k, top, hx:].astype(F32)
            out.append((sums[2 * k] + fold(w * w * energy)))
            out.append((sums[2 * k + 1] + fold(e * e * edge)))
        return tuple(out)

    sc, ss = spec[hy : hy + 8, :hx], spec[hy : hy + 8, hx:]
    sc, ss = sc * sc, ss * ss
    first_row = sub[:8] == 0
    bottom = jnp.where(first_row, sc + jnp.where(lane[:8] > 0, ss, 0.0), 0.0)
    corner = jnp.where(jnp.logical_and(first_row[:, :128], lane_one[:8] == 0), ss[:, :128], 0.0)
    sums = []
    for k in range(LEVELS):
        w = band[k, hy:, :hx].astype(F32)
        e = band[k, hy:, hx:].astype(F32)
        sums += [w * w * bottom, e * e * corner]
    sums = lax.fori_loop(0, hy // strip, powers, tuple(sums), unroll=2)
    levels = []
    for k in range(LEVELS):
        both = jnp.concatenate([sums[2 * k], sums[2 * k + 1]], axis=1)
        power = jnp.sum(jnp.sum(both, axis=0, keepdims=True), axis=1, keepdims=True) / float(height * width)
        levels.append(coef[k][2][:, :1] / jnp.sqrt(power + 1e-06))
    level = [jnp.broadcast_to(v, (1, hx + 128)) for v in levels]

    last = sum(level[k] * band[k, hy:, :].astype(F32) for k in range(LEVELS))[:1]

    def apply(i, carry):
        r = pl.multiple_of(i * strip, strip)
        top = pl.ds(r, strip)
        low = pl.ds(hy + r, strip)
        a = level[0] * band[0, top, :].astype(F32)
        for k in range(1, LEVELS):
            a += level[k] * band[k, top, :].astype(F32)

        def right_of(v):
            begin = jnp.where(lane_one == 0, v[:, hx:], v[:, :128])
            return jnp.concatenate([begin, v[:, 128:hx]], axis=1) if hx > 128 else begin

        gain[top, :hx] = (a[:, :hx] * spec[top, :hx]).astype(BF16)
        gain[top, hx:] = (right_of(a) * spec[top, hx:]).astype(BF16)
        wide = lax.broadcasted_iota(jnp.int32, (strip, hx + 128), 0) + r
        b = jnp.where(wide == 0, last, a)
        gain[low, :hx] = (b[:, :hx] * spec[low, :hx]).astype(BF16)
        gain[low, hx:] = (right_of(b) * spec[low, hx:]).astype(BF16)
        return carry

    lax.fori_loop(0, hy // strip, apply, 0, unroll=2)

    back = dot(jnp.concatenate([rows_t[0], rows_t[1]], axis=0), gain[...])
    b_hi, b_lo = split(back[:rows] + back[rows:])
    field = dot(jnp.concatenate([b_hi, b_lo], axis=0), tx[...])
    raw = (steady[...] + (field[:rows] + field[rows:])) * mask[...]
    mean[...] = raw
    fc[...] = raw.astype(BF16)

    sends = [
        pltpu.make_async_remote_copy(
            src_ref=fc, dst_ref=arrived.at[d - 1], send_sem=mem_send.at[d - 1], recv_sem=mem_recv.at[d - 1],
            device_id={"member": (m + d) % members}, device_id_type=pl.DeviceIdType.MESH,
        )
        for d in range(1, members)
    ]
    for send in sends:
        send.start()

    for c in range(chunks):
        for d in range(1, depth):
            both_ways(d, lambda up: along(up, d, c).wait_send())
        if pair > 1:
            for zb in range(depth):
                across(zb, c).wait_send()

    @pl.when(t < tiles - 1)
    def _():
        after.wait_send()

    @pl.when(t > 0)
    def _():
        before.wait_send()

    total = mean[...]
    for d in range(1, members):
        sends[d - 1].wait_recv()
        total += arrived[d - 1].astype(F32)
    mean[...] = total * (1.0 / members)
    for send in sends:
        send.wait_send()


def shards(tables, tiles, members, noise, observed, row_shift, col_shift, rain_mask, autocorr, level_scale):
    _, rows, width = noise.shape
    height = rows * tiles
    pair = 2 if tiles % 2 == 0 else 1
    depth, chunks = tiles // pair, rows // chunk_of(rows)
    any_space = pl.BlockSpec(memory_space=pl.ANY)
    dma = pltpu.SemaphoreType.DMA
    peers = max(members - 1, 1)
    fields = pl.pallas_call(
        functools.partial(kernel, tiles, pair, members),
        out_shape=(pltpu.VMEM((1, rows, width), BF16), pltpu.VMEM((rows, width), F32)),
        in_specs=[any_space] * 12,
        out_specs=(pl.BlockSpec(memory_space=pltpu.VMEM),) * 2,
        scratch_shapes=[
            pltpu.VMEM((rows, width), F32),
            pltpu.VMEM(observed.shape, BF16),
            pltpu.VMEM((rows, width), jnp.int32),
            pltpu.VMEM((rows, width), jnp.int32),
            pltpu.VMEM((height, height), BF16),
            pltpu.VMEM((width, width), BF16),
            pltpu.VMEM((width, width), BF16),
            pltpu.VMEM((width, width), BF16),
            pltpu.VMEM((2, rows, height), BF16),
            pltpu.VMEM(tables[-1].shape, BF16),
            pltpu.VMEM((height, width), BF16),
            pltpu.VMEM((rows + 2 * PAD, width), F32),
            pltpu.VMEM((2 * HALO + 1, rows + 2 * PAD, width), F32),
            pltpu.VMEM((rows, width), F32),
            pltpu.VMEM((rows, width), F32),
            pltpu.VMEM((height, width), F32),
            pltpu.VMEM((height, width), BF16),
            pltpu.VMEM((peers, rows, width), BF16),
            pltpu.SMEM(rain_mask.shape[::-1], jnp.int32),
            pltpu.SMEM(autocorr.shape, F32),
            pltpu.SMEM(level_scale.shape, F32),
            dma((13,)),
            dma((2, depth, chunks)),
            dma((depth, chunks)),
            dma((tiles, chunks)),
            dma((2,)),
            dma((2,)),
            dma((peers,)),
            dma((peers,)),
        ],
        compiler_params=pltpu.CompilerParams(
            collective_id=0, has_side_effects=True, vmem_limit_bytes=67043328 - 4 * 64 * 1024
        ),
        name="nowcast",
    )(noise, observed, row_shift, col_shift, rain_mask.T, autocorr, level_scale, *tables)
    return pl.pallas_call(
        write_out,
        out_shape=(
            jax.ShapeDtypeStruct((1, rows, width), BF16),
            jax.ShapeDtypeStruct((rows, width), F32),
        ),
        in_specs=[pl.BlockSpec(memory_space=pltpu.VMEM)] * 2,
        out_specs=(any_space, any_space),
        scratch_shapes=[dma((2,))],
        compiler_params=pltpu.CompilerParams(vmem_limit_bytes=1024 * 1024),
        name="write_out",
    )(*fields)


def solution(mesh):
    tiles, members = mesh.shape["tile"], mesh.shape["member"]
    in_specs = (
        P("member", "tile", None),
        P(None, None, "tile", None),
        P("tile", None),
        P("tile", None),
        P("tile", None),
        P(),
        P(),
    )
    out_specs = (P("member", "tile", None), P("tile", None))

    def program(noise, observed, *rest):
        height, width = noise.shape[1:]

        def halves(table):
            high = table.astype(jnp.bfloat16)
            return high, (table - high.astype(np.float64)).astype(jnp.bfloat16)

        basis_y, basis_x = real_basis(height), real_basis(width)
        tables = (
            basis_y.astype(jnp.bfloat16),
            basis_x.astype(jnp.bfloat16),
            np.stack(halves(np.ascontiguousarray(basis_x.T))),
            np.stack(halves(np.ascontiguousarray(basis_y.T))),
            band_table(height, width).astype(jnp.bfloat16),
        )
        body = functools.partial(shards, tables, tiles, members)
        return jax.shard_map(body, mesh=mesh, in_specs=in_specs, out_specs=out_specs, check_vma=False)(
            noise, observed, *rest
        )

    return program
```

```python
import functools
import math

import jax
import jax.numpy as jnp
import numpy as np
from jax import lax
from jax.experimental import pallas as pl
from jax.experimental.pallas import tpu as pltpu
from jax.sharding import PartitionSpec as P

LEVELS = 6
HALO = 4
PAD = 8
F32 = jnp.float32
BF16 = jnp.bfloat16
PLAN = (
    (
        ((0, 0, 1), (0, 2, 0), (1, 0, 1), (1, 2, 0), (0, 1, 1), (1, 1, 1)),
        (
            (1, 0, 0, ((2, 0), (0, 1))),
            (1, 0, 1, ((0, 1),)),
            (3, 0, 1, ((0, 1), (1, 0))),
            (3, 1, 0, ((1, 0),)),
            (3, 0, 0, ((1, 0),)),
        ),
    ),
    (
        ((0, 0, 0), (1, 3, 0), (1, 0, 0), (0, 3, 0), (0, 1, 1), (1, 1, 1)),
        (
            (2, 0, 1, ((0, 0), (1, 1))),
            (2, 0, 0, ((0, 0), (1, 1))),
            (0, 1, 0, ((1, 1), (3, 0))),
            (0, 1, 1, ((3, 0), (1, 1))),
            (1, 1, 0, ((2, 0),)),
        ),
    ),
    (
        ((1, 1, 0), (1, 2, 1), (0, 3, 0), (1, 3, 0), (0, 2, 1), (0, 1, 0)),
        (
            (2, 1, 1, ((0, 0),)),
            (0, 0, 0, ((3, 0), (2, 1))),
            (2, 1, 0, ((0, 0), (3, 0))),
            (0, 0, 1, ((2, 1), (3, 0))),
            (3, 1, 1, ((1, 0),)),
        ),
    ),
    (
        ((1, 0, 0), (0, 0, 1), (1, 3, 1), (0, 3, 1), (0, 0, 0), (1, 2, 1)),
        (
            (3, 1, 1, ((2, 1),)),
            (2, 0, 1, ((3, 1),)),
            (3, 1, 0, ((2, 1), (2, 0))),
            (1, 0, 1, ((2, 1), (2, 0), (3, 1))),
            (1, 0, 0, ((3, 1),)),
        ),
    ),
)


def real_basis(length):
    half = length // 2
    positions = np.arange(length)
    angles = 2.0 * math.pi * (np.outer(np.arange(half), positions) % length) / length
    cosines = np.cos(angles) * math.sqrt(2.0 / length)
    sines = np.sin(angles) * math.sqrt(2.0 / length)
    cosines[0] = 1.0 / math.sqrt(length)
    sines[0] = (1.0 - 2.0 * (positions % 2)) / math.sqrt(length)
    return np.concatenate([cosines, sines], axis=0)


def band_table(height, width):
    freq_y = np.arange(height // 2 + PAD)[:, None] / height
    freq_x = np.arange(width // 2 + 128)[None, :] / width
    longest = max(height, width)
    log_radius = np.log(longest * np.sqrt(freq_y * freq_y + freq_x * freq_x) + 1.0)
    spacing = math.log(longest / 2.0) / (LEVELS - 1)
    offsets = log_radius[None] - spacing * np.arange(LEVELS)[:, None, None]
    bumps = np.exp(-(offsets * offsets) / (2.0 * (0.6 * spacing) ** 2))
    return bumps / np.sum(bumps, axis=0, keepdims=True)


def chunk_of(rows):
    return rows // 2 if rows % 32 == 0 else rows


def split(value):
    high = value.astype(BF16)
    return high, (value - high.astype(F32)).astype(BF16)


def planned(tiles, pair, chunks):
    chunk_count = 1 + max(send[0] for first, _ in PLAN for send in first)
    return pair == 2 and tiles == 2 * len(PLAN) and chunks == chunk_count


def plan_slots():
    return 2 + max(len(relays) for _, relays in PLAN)


def targets(t, tiles, pair, chunks):
    near = {u for u in (t - 1, t + 1) if 0 <= u < tiles}
    z, x = divmod(t, pair)
    if planned(tiles, pair, chunks):
        first, relays = PLAN[z]
        ends = {(a, b) for _, a, b in first} | {end for relay in relays for end in relay[3]}
        return near | {a * pair + (x ^ b) for a, b in ends}
    return near | {u * pair + x for u in range(tiles // pair) if u != z} | ({z * pair + 1 - x} if pair > 1 else set())


def dot(a, b):
    return jnp.dot(a, b, preferred_element_type=F32)


def coefficients(ac, scale, k, width):
    g1 = jnp.full((1, width), ac[0, k], F32)
    g2 = jnp.full((1, width), ac[1, k], F32)
    s = jnp.full((1, width), scale[k], F32)
    den = 1.0 - g1 * g1
    one = g1 * (1.0 - g2) / den
    two = (g2 - g1 * g1) / den
    innovation = jnp.sqrt(1.0 - one * g1 - two * g2)
    return s * one, s * two, s * innovation


def write_out(fc, mean, fc_hbm, mean_hbm, sem):
    copies = [pltpu.make_async_copy(a, b, sem.at[i]) for i, (a, b) in enumerate([(fc, fc_hbm), (mean, mean_hbm)])]
    for copy in copies:
        copy.start()
    for copy in copies:
        copy.wait()


def kernel(
    tiles, pair, members,
    noise_hbm, obs_hbm, row_hbm, col_hbm, rain_hbm, ac_hbm, scale_hbm, ty_hbm, tx_hbm, txt_hbm, tyt_hbm, band_hbm,
    fc_out, mean,
    noise, obs, shift, ty, tx, txt, rows_t, band,
    xg, pad, shifted, steady, mask, spec, gain, arrived, rain, ac, scale,
    load_sem, send_sem, cross_sem, plan_sem, recv_sem, halo_send, halo_recv, mem_send, mem_recv,
):
    fc = fc_out.at[0]
    rows, width = noise.shape
    height = rows * tiles
    hy, hx = height // 2, width // 2
    depth = tiles // pair
    size = chunk_of(rows)
    chunks = rows // size
    plan = planned(tiles, pair, chunks)
    t = lax.axis_index("tile")
    m = lax.axis_index("member")
    z = t // pair
    x = t % pair

    sources = [
        (noise_hbm.at[0], noise), (txt_hbm, txt),
        (rain_hbm, rain), (ac_hbm, ac), (scale_hbm, scale), (obs_hbm, obs),
        (ty_hbm, ty), (band_hbm, band),
        (tyt_hbm.at[:, pl.ds(pl.multiple_of(t * rows, rows), rows), :], rows_t), (tx_hbm, tx),
    ]
    loads = [pltpu.make_async_copy(a, b, load_sem.at[i]) for i, (a, b) in enumerate(sources)]
    moves = [pltpu.make_async_copy(a, shift.at[i], load_sem.at[len(sources)]) for i, a in enumerate((row_hbm, col_hbm))]
    both_moves = pltpu.make_async_copy(shift, shift, load_sem.at[len(sources)])
    for load in loads[:2]:
        load.start()

    barrier = pltpu.get_barrier_semaphore()
    ends = [targets(u, tiles, pair, chunks) for u in range(tiles)]
    greeted = 0
    if plan:
        for u in range(tiles):
            greeted = greeted + (t == u).astype(jnp.int32) * len(ends[u])

            @pl.when(t == u)
            def _():
                for v in range(tiles):
                    if u in ends[v]:
                        pl.semaphore_signal(barrier, inc=1, device_id={"tile": v}, device_id_type=pl.DeviceIdType.MESH)
    else:
        near = sorted({pair * d for d in range(1, depth)} | {1})
        for step in [sign * d for d in near for sign in (-1, 1)]:
            there = jnp.logical_and(t + step >= 0, t + step < tiles)
            greeted = greeted + there.astype(jnp.int32)

            @pl.when(there)
            def _():
                pl.semaphore_signal(barrier, inc=1, device_id={"tile": t + step}, device_id_type=pl.DeviceIdType.MESH)

    for d in range(1, members):
        pl.semaphore_signal(
            barrier, inc=1, device_id={"member": (m + d) % members}, device_id_type=pl.DeviceIdType.MESH
        )

    for load in loads[2:6] + moves + loads[6:]:
        load.start()
    for load in loads[:2]:
        load.wait()
    own = pl.multiple_of(t * rows, rows)
    n_hi, n_lo = split(noise[...])
    first = dot(jnp.concatenate([n_hi, n_lo], axis=0), txt[0])
    xg[pl.ds(own, rows), :] = (first[:rows] + first[rows:] + dot(n_hi, txt[1])).astype(BF16)
    pl.semaphore_wait(barrier, greeted + members - 1)

    def part(block, c):
        return xg.at[pl.ds(pl.multiple_of(block * rows + c * size, size), size), :]

    def along(up, d, c):
        mine = part(t, c)
        return pltpu.make_async_remote_copy(
            src_ref=mine, dst_ref=mine, send_sem=send_sem.at[up, d, c], recv_sem=recv_sem.at[t, c],
            device_id={"tile": t + pair * (d if up else -d)}, device_id_type=pl.DeviceIdType.MESH,
        )

    def across(zb, c):
        block = part(zb * pair + x, c)
        return pltpu.make_async_remote_copy(
            src_ref=block, dst_ref=block, send_sem=cross_sem.at[zb, c], recv_sem=recv_sem.at[zb * pair + x, c],
            device_id={"tile": z * pair + 1 - x}, device_id_type=pl.DeviceIdType.MESH,
        )

    def arrival(block, c):
        pltpu.make_async_copy(part(block, c), part(block, c), recv_sem.at[block, c]).wait()

    def both_ways(d, act):
        @pl.when(z + d < depth)
        def _():
            act(1)

        @pl.when(z - d >= 0)
        def _():
            act(0)

    def column(other):
        return 1 - x if other else x

    def message(number, block_z, block_other, c, end_z, end_other):
        block = block_z * pair + column(block_other)
        mine = part(block, c)
        return pltpu.make_async_remote_copy(
            src_ref=mine, dst_ref=mine, send_sem=plan_sem.at[0], recv_sem=plan_sem.at[number],
            device_id={"tile": end_z * pair + column(end_other)}, device_id_type=pl.DeviceIdType.MESH,
        )

    def slot(end_z, block_z, block_other, c):
        passed = [relay[:3] for relay in PLAN[end_z][1]]
        key = (block_z, block_other, c)
        return 2 + passed.index(key) if key in passed else 1

    def landed(number, count):
        bulk = xg.at[pl.ds(0, count * size), :]
        pltpu.make_async_copy(bulk, bulk, plan_sem.at[number]).wait()

    def at_level(act):
        for k in range(depth):
            pl.when(z == k)(functools.partial(act, k, *PLAN[k]))

    def first_sends(k, first, relays):
        for c, a, b in first:
            message(slot(a, k, b, c), k, 0, c, a, b).start()

    def pass_on(k, first, relays):
        for i, (block_z, block_other, c, goals) in enumerate(relays):
            landed(2 + i, 1)
            for a, b in goals:
                message(slot(a, block_z, block_other ^ b, c), block_z, block_other, c, a, b).start()

    def last_arrivals(k, first, relays):
        landed(1, (tiles - 1) * chunks - len(relays))

    def sends_done(k, first, relays):
        landed(0, len(first) + sum(len(relay[3]) for relay in relays))

    if plan:
        at_level(first_sends)
    else:
        for c in range(chunks):
            if pair > 1:
                across(z, c).start()
            for d in range(depth - 1, 0, -1):
                both_ways(d, lambda up: along(up, d, c).start())

    def relay(s):
        def take(up, c):
            zb = z + s if up else z - s
            arrival(zb * pair + x, c)
            if pair > 1:
                across(zb, c).start()

        for c in range(chunks):
            both_ways(s, lambda up: take(up, c))

    for load in loads[2:6]:
        load.wait()
    coef = [coefficients(ac, scale, k, width) for k in range(LEVELS)]
    for g in range(rows // 16):
        span = pl.ds(16 * g, 16)
        total = jnp.zeros((16, width), F32)
        for k in range(LEVELS):
            total += coef[k][0] * obs[0, k, span, :].astype(F32) + coef[k][1] * obs[1, k, span, :].astype(F32)
        pad[pl.ds(PAD + 16 * g, 16), :] = total
    for i in range(rows // 8):
        for j in range(width // 128):
            mask[8 * i : 8 * i + 8, 128 * j : 128 * j + 128] = jnp.full((8, 128), rain[j, i].astype(F32), F32)

    after = pltpu.make_async_remote_copy(
        src_ref=pad.at[pl.ds(rows, PAD), :], dst_ref=pad.at[pl.ds(0, PAD), :],
        send_sem=halo_send.at[0], recv_sem=halo_recv.at[0],
        device_id={"tile": t + 1}, device_id_type=pl.DeviceIdType.MESH,
    )
    before = pltpu.make_async_remote_copy(
        src_ref=pad.at[pl.ds(PAD, PAD), :], dst_ref=pad.at[pl.ds(rows + PAD, PAD), :],
        send_sem=halo_send.at[1], recv_sem=halo_recv.at[1],
        device_id={"tile": t - 1}, device_id_type=pl.DeviceIdType.MESH,
    )

    @pl.when(t < tiles - 1)
    def _():
        after.start()

    @pl.when(t == tiles - 1)
    def _():
        pad[rows + PAD :, :] = jnp.zeros((PAD, width), F32)

    @pl.when(t > 0)
    def _():
        before.start()

    @pl.when(t == 0)
    def _():
        pad[:PAD, :] = jnp.zeros((PAD, width), F32)

    def shift_columns(start, count):
        lane = lax.broadcasted_iota(jnp.int32, (count, width), 1)
        value = pad[start : start + count, :]
        for dx in range(-HALO, HALO + 1):
            moved = pltpu.roll(value, dx % width, 1) if dx else value
            if dx > 0:
                moved = jnp.where(lane >= dx, moved, 0.0)
            if dx < 0:
                moved = jnp.where(lane < width + dx, moved, 0.0)
            shifted[dx + HALO, start : start + count, :] = moved

    def gather_rows(start, stop):
        for g in range(start, stop):
            span = pl.ds(8 * g, 8)
            code = shift[0, span, :] * (2 * HALO + 1) + shift[1, span, :]
            total = jnp.zeros((8, width), F32)
            for dy in range(-HALO, HALO + 1):
                for dx in range(-HALO, HALO + 1):
                    total = jnp.where(
                        code == dy * (2 * HALO + 1) + dx,
                        shifted[dx + HALO, 8 * g + PAD - dy : 8 * g + PAD - dy + 8, :],
                        total,
                    )
            steady[span, :] = total

    groups = rows // 8
    shift_columns(PAD, rows)
    both_moves.wait()
    gather_rows(1, groups - 1)

    if plan:
        at_level(pass_on)
    else:
        for s in range(1, depth):
            relay(s)

    @pl.when(t > 0)
    def _():
        after.wait_recv()

    @pl.when(t < tiles - 1)
    def _():
        before.wait_recv()

    shift_columns(0, PAD)
    shift_columns(rows + PAD, PAD)
    gather_rows(0, 1)
    gather_rows(max(groups - 1, 1), groups)
    for load in loads[6:]:
        load.wait()
    if plan:
        at_level(last_arrivals)
    elif pair > 1:
        for zb in range(depth):
            for c in range(chunks):
                arrival(zb * pair + 1 - x, c)

    spec[...] = dot(ty[...], xg[...])
    strip = 16
    lane = lax.broadcasted_iota(jnp.int32, (strip, hx), 1)
    lane_one = lax.broadcasted_iota(jnp.int32, (strip, 128), 1)
    sub = lax.broadcasted_iota(jnp.int32, (strip, hx), 0)

    def fold(value):
        return value[:8] + value[8:]

    def powers(i, sums):
        r = pl.multiple_of(i * strip, strip)
        top = pl.ds(r, strip)
        low = pl.ds(hy + r, strip)
        cc, cs = spec[top, :hx], spec[top, hx:]
        sc, ss = spec[low, :hx], spec[low, hx:]
        cc, cs, sc, ss = cc * cc, cs * cs, sc * sc, ss * ss
        inner = sub + r > 0
        sc = jnp.where(inner, sc, 0.0)
        ss = jnp.where(inner, ss, 0.0)
        right = cs + ss
        energy = cc + sc + jnp.where(lane > 0, right, 0.0)
        edge = jnp.where(lane_one == 0, right[:, :128], 0.0)
        out = []
        for k in range(LEVELS):
            w = band[k, top, :hx].astype(F32)
            e = band[k, top, hx:].astype(F32)
            out.append((sums[2 * k] + fold(w * w * energy)))
            out.append((sums[2 * k + 1] + fold(e * e * edge)))
        return tuple(out)

    sc, ss = spec[hy : hy + 8, :hx], spec[hy : hy + 8, hx:]
    sc, ss = sc * sc, ss * ss
    first_row = sub[:8] == 0
    bottom = jnp.where(first_row, sc + jnp.where(lane[:8] > 0, ss, 0.0), 0.0)
    corner = jnp.where(jnp.logical_and(first_row[:, :128], lane_one[:8] == 0), ss[:, :128], 0.0)
    sums = []
    for k in range(LEVELS):
        w = band[k, hy:, :hx].astype(F32)
        e = band[k, hy:, hx:].astype(F32)
        sums += [w * w * bottom, e * e * corner]
    sums = lax.fori_loop(0, hy // strip, powers, tuple(sums), unroll=2)
    levels = []
    for k in range(LEVELS):
        both = jnp.concatenate([sums[2 * k], sums[2 * k + 1]], axis=1)
        power = jnp.sum(jnp.sum(both, axis=0, keepdims=True), axis=1, keepdims=True) / float(height * width)
        levels.append(coef[k][2][:, :1] / jnp.sqrt(power + 1e-06))
    level = [jnp.broadcast_to(v, (1, hx + 128)) for v in levels]

    last = sum(level[k] * band[k, hy:, :].astype(F32) for k in range(LEVELS))[:1]

    def apply(i, carry):
        r = pl.multiple_of(i * strip, strip)
        top = pl.ds(r, strip)
        low = pl.ds(hy + r, strip)
        a = level[0] * band[0, top, :].astype(F32)
        for k in range(1, LEVELS):
            a += level[k] * band[k, top, :].astype(F32)

        def right_of(v):
            begin = jnp.where(lane_one == 0, v[:, hx:], v[:, :128])
            return jnp.concatenate([begin, v[:, 128:hx]], axis=1) if hx > 128 else begin

        gain[top, :hx] = (a[:, :hx] * spec[top, :hx]).astype(BF16)
        gain[top, hx:] = (right_of(a) * spec[top, hx:]).astype(BF16)
        wide = lax.broadcasted_iota(jnp.int32, (strip, hx + 128), 0) + r
        b = jnp.where(wide == 0, last, a)
        gain[low, :hx] = (b[:, :hx] * spec[low, :hx]).astype(BF16)
        gain[low, hx:] = (right_of(b) * spec[low, hx:]).astype(BF16)
        return carry

    lax.fori_loop(0, hy // strip, apply, 0, unroll=2)

    back = dot(jnp.concatenate([rows_t[0], rows_t[1]], axis=0), gain[...])
    b_hi, b_lo = split(back[:rows] + back[rows:])
    field = dot(jnp.concatenate([b_hi, b_lo], axis=0), tx[...])
    raw = (steady[...] + (field[:rows] + field[rows:])) * mask[...]
    mean[...] = raw
    fc[...] = raw.astype(BF16)

    sends = [
        pltpu.make_async_remote_copy(
            src_ref=fc, dst_ref=arrived.at[d - 1], send_sem=mem_send.at[0], recv_sem=mem_recv.at[0],
            device_id={"member": (m + d) % members}, device_id_type=pl.DeviceIdType.MESH,
        )
        for d in range(1, members)
    ]
    for send in sends:
        send.start()

    if plan:
        at_level(sends_done)
    else:
        for c in range(chunks):
            for d in range(1, depth):
                both_ways(d, lambda up: along(up, d, c).wait_send())
            if pair > 1:
                for zb in range(depth):
                    across(zb, c).wait_send()

    @pl.when(t < tiles - 1)
    def _():
        after.wait_send()

    @pl.when(t > 0)
    def _():
        before.wait_send()

    everyone = pltpu.make_async_copy(arrived, arrived, mem_recv.at[0])
    if members > 1:
        everyone.wait()
    total = mean[...]
    for d in range(1, members):
        total += arrived[d - 1].astype(F32)
    mean[...] = total * (1.0 / members)
    if members > 1:
        pltpu.make_async_copy(arrived, arrived, mem_send.at[0]).wait()


def shards(tables, tiles, members, noise, observed, row_shift, col_shift, rain_mask, autocorr, level_scale):
    _, rows, width = noise.shape
    height = rows * tiles
    pair = 2 if tiles % 2 == 0 else 1
    depth, chunks = tiles // pair, rows // chunk_of(rows)
    any_space = pl.BlockSpec(memory_space=pl.ANY)
    dma = pltpu.SemaphoreType.DMA
    plan = planned(tiles, pair, chunks)
    peers = max(members - 1, 1)
    fields = pl.pallas_call(
        functools.partial(kernel, tiles, pair, members),
        out_shape=(pltpu.VMEM((1, rows, width), BF16), pltpu.VMEM((rows, width), F32)),
        in_specs=[any_space] * 12,
        out_specs=(pl.BlockSpec(memory_space=pltpu.VMEM),) * 2,
        scratch_shapes=[
            pltpu.VMEM((rows, width), F32),
            pltpu.VMEM(observed.shape, BF16),
            pltpu.VMEM((2, rows, width), jnp.int32),
            pltpu.VMEM((height, height), BF16),
            pltpu.VMEM((width, width), BF16),
            pltpu.VMEM((2, width, width), BF16),
            pltpu.VMEM((2, rows, height), BF16),
            pltpu.VMEM(tables[-1].shape, BF16),
            pltpu.VMEM((height, width), BF16),
            pltpu.VMEM((rows + 2 * PAD, width), F32),
            pltpu.VMEM((2 * HALO + 1, rows + 2 * PAD, width), F32),
            pltpu.VMEM((rows, width), F32),
            pltpu.VMEM((rows, width), F32),
            pltpu.VMEM((height, width), F32),
            pltpu.VMEM((height, width), BF16),
            pltpu.VMEM((peers, rows, width), BF16),
            pltpu.SMEM(rain_mask.shape[::-1], jnp.int32),
            pltpu.SMEM(autocorr.shape, F32),
            pltpu.SMEM(level_scale.shape, F32),
            dma((11,)),
            *([dma((1,))] * 2 if plan else [dma((2, depth, chunks)), dma((depth, chunks))]),
            dma((plan_slots(),)) if plan else dma((1,)),
            dma((1,)) if plan else dma((tiles, chunks)),
            dma((2,)),
            dma((2,)),
            dma((1,)),
            dma((1,)),
        ],
        compiler_params=pltpu.CompilerParams(
            collective_id=0, has_side_effects=True, vmem_limit_bytes=67043328 - 4 * 64 * 1024
        ),
        name="nowcast",
    )(noise, observed, row_shift, col_shift, rain_mask.T, autocorr, level_scale, *tables)
    return pl.pallas_call(
        write_out,
        out_shape=(
            jax.ShapeDtypeStruct((1, rows, width), BF16),
            jax.ShapeDtypeStruct((rows, width), F32),
        ),
        in_specs=[pl.BlockSpec(memory_space=pltpu.VMEM)] * 2,
        out_specs=(any_space, any_space),
        scratch_shapes=[dma((2,))],
        compiler_params=pltpu.CompilerParams(vmem_limit_bytes=1024 * 1024),
        name="write_out",
    )(*fields)


def solution(mesh):
    tiles, members = mesh.shape["tile"], mesh.shape["member"]
    in_specs = (
        P("member", "tile", None),
        P(None, None, "tile", None),
        P("tile", None),
        P("tile", None),
        P("tile", None),
        P(),
        P(),
    )
    out_specs = (P("member", "tile", None), P("tile", None))

    def program(noise, observed, *rest):
        height, width = noise.shape[1:]

        def halves(table):
            high = table.astype(jnp.bfloat16)
            return high, (table - high.astype(np.float64)).astype(jnp.bfloat16)

        basis_y, basis_x = real_basis(height), real_basis(width)
        tables = (
            basis_y.astype(jnp.bfloat16),
            basis_x.astype(jnp.bfloat16),
            np.stack(halves(np.ascontiguousarray(basis_x.T))),
            np.stack(halves(np.ascontiguousarray(basis_y.T))),
            band_table(height, width).astype(jnp.bfloat16),
        )
        body = functools.partial(shards, tables, tiles, members)
        return jax.shard_map(body, mesh=mesh, in_specs=in_specs, out_specs=out_specs, check_vma=False)(
            noise, observed, *rest
        )

    return program
```

```python
import functools
import math

import jax
import jax.numpy as jnp
import numpy as np
from jax import lax
from jax.experimental import pallas as pl
from jax.experimental.pallas import tpu as pltpu
from jax.sharding import PartitionSpec as P

LEVELS = 6
HALO = 4
PAD = 8
F32 = jnp.float32
BF16 = jnp.bfloat16
PLAN = (
    (
        ((1, 0, 1), (1, 1, 0), (0, 0, 1), (0, 1, 0)),
        (
            (0, 1, 1, ((1, 0),)),
            (2, 0, 1, ((0, 1), (1, 0))),
            (2, 0, 0, ((0, 1), (1, 0))),
            (3, 0, 0, ((0, 1),)),
        ),
    ),
    (
        ((1, 3, 0), (1, 2, 0), (0, 2, 0), (0, 1, 1), (1, 0, 0), (1, 1, 1), (0, 0, 0)),
        (
            (0, 0, 1, ((3, 0),)),
            (0, 0, 0, ((1, 1), (3, 0))),
            (1, 1, 0, ((3, 0), (0, 0))),
            (1, 1, 1, ((0, 0), (3, 0))),
            (0, 1, 1, ((2, 0),)),
            (3, 0, 0, ((2, 0), (1, 1))),
            (0, 1, 0, ((2, 0),)),
        ),
    ),
    (
        ((1, 0, 0), (1, 2, 1), (0, 2, 1), (1, 3, 0), (0, 0, 0), (0, 3, 0)),
        (
            (2, 1, 1, ((1, 0),)),
            (2, 1, 0, ((1, 0),)),
            (3, 1, 1, ((0, 0), (3, 0), (1, 0))),
            (1, 0, 0, ((2, 1), (3, 0))),
            (3, 0, 1, ((1, 0),)),
        ),
    ),
    (
        ((0, 0, 0), (0, 3, 1), (1, 2, 1), (0, 1, 0), (1, 0, 0), (1, 2, 0)),
        (
            (2, 0, 1, ((3, 1),)),
            (3, 1, 0, ((2, 0),)),
            (2, 0, 0, ((3, 1),)),
            (1, 0, 1, ((2, 1),)),
            (0, 0, 1, ((2, 0), (3, 1))),
            (0, 0, 0, ((3, 1), (2, 0))),
        ),
    ),
)


def real_basis(length):
    half = length // 2
    positions = np.arange(length)
    angles = 2.0 * math.pi * (np.outer(np.arange(half), positions) % length) / length
    cosines = np.cos(angles) * math.sqrt(2.0 / length)
    sines = np.sin(angles) * math.sqrt(2.0 / length)
    cosines[0] = 1.0 / math.sqrt(length)
    sines[0] = (1.0 - 2.0 * (positions % 2)) / math.sqrt(length)
    return np.concatenate([cosines, sines], axis=0)


def band_table(height, width):
    freq_y = np.arange(height // 2 + PAD)[:, None] / height
    freq_x = np.arange(width // 2 + 128)[None, :] / width
    longest = max(height, width)
    log_radius = np.log(longest * np.sqrt(freq_y * freq_y + freq_x * freq_x) + 1.0)
    spacing = math.log(longest / 2.0) / (LEVELS - 1)
    offsets = log_radius[None] - spacing * np.arange(LEVELS)[:, None, None]
    bumps = np.exp(-(offsets * offsets) / (2.0 * (0.6 * spacing) ** 2))
    return bumps / np.sum(bumps, axis=0, keepdims=True)


def chunk_of(rows):
    return rows // 2 if rows % 32 == 0 else rows


def split(value):
    high = value.astype(BF16)
    return high, (value - high.astype(F32)).astype(BF16)


def planned(tiles, pair, chunks):
    chunk_count = 1 + max(send[0] for first, _ in PLAN for send in first)
    return pair == 2 and tiles == 2 * len(PLAN) and chunks == chunk_count


def plan_slots():
    return 2 + max(len(relays) for _, relays in PLAN)


def targets(t, tiles, pair, chunks):
    near = {u for u in (t - 1, t + 1) if 0 <= u < tiles}
    z, x = divmod(t, pair)
    if planned(tiles, pair, chunks):
        first, relays = PLAN[z]
        ends = {(a, b) for _, a, b in first} | {end for relay in relays for end in relay[3]}
        return near | {a * pair + (x ^ b) for a, b in ends}
    return near | {u * pair + x for u in range(tiles // pair) if u != z} | ({z * pair + 1 - x} if pair > 1 else set())


def dot(a, b):
    return jnp.dot(a, b, preferred_element_type=F32)


def coefficients(ac, scale, k, width):
    g1 = jnp.full((1, width), ac[0, k], F32)
    g2 = jnp.full((1, width), ac[1, k], F32)
    s = jnp.full((1, width), scale[k], F32)
    den = 1.0 - g1 * g1
    one = g1 * (1.0 - g2) / den
    two = (g2 - g1 * g1) / den
    innovation = jnp.sqrt(1.0 - one * g1 - two * g2)
    return s * one, s * two, s * innovation


def write_out(fc, mean, fc_hbm, mean_hbm, sem):
    copies = [pltpu.make_async_copy(a, b, sem.at[i]) for i, (a, b) in enumerate([(fc, fc_hbm), (mean, mean_hbm)])]
    for copy in copies:
        copy.start()
    for copy in copies:
        copy.wait()


def kernel(
    tiles, pair, members,
    noise_hbm, obs_hbm, row_hbm, col_hbm, rain_hbm, ac_hbm, scale_hbm, ty_hbm, tx_hbm, txt_hbm, tyt_hbm, band_hbm,
    fc_out, mean,
    noise, obs, shift, ty, tx, txt, rows_t, band,
    xg, pad, shifted, steady, mask, spec, gain, arrived, rain, ac, scale,
    load_sem, send_sem, cross_sem, plan_sem, recv_sem, halo_send, halo_recv, mem_send, mem_recv,
):
    fc = fc_out.at[0]
    rows, width = noise.shape
    height = rows * tiles
    hy, hx = height // 2, width // 2
    depth = tiles // pair
    size = chunk_of(rows)
    chunks = rows // size
    plan = planned(tiles, pair, chunks)
    t = lax.axis_index("tile")
    m = lax.axis_index("member")
    z = t // pair
    x = t % pair

    sources = [
        (noise_hbm.at[0], noise), (txt_hbm, txt),
        (rain_hbm, rain), (ac_hbm, ac), (scale_hbm, scale), (obs_hbm, obs),
        (ty_hbm, ty), (band_hbm, band),
        (tyt_hbm.at[:, pl.ds(pl.multiple_of(t * rows, rows), rows), :], rows_t), (tx_hbm, tx),
    ]
    loads = [pltpu.make_async_copy(a, b, load_sem.at[i]) for i, (a, b) in enumerate(sources)]
    moves = [pltpu.make_async_copy(a, shift.at[i], load_sem.at[len(sources)]) for i, a in enumerate((row_hbm, col_hbm))]
    both_moves = pltpu.make_async_copy(shift, shift, load_sem.at[len(sources)])
    for load in loads[:2]:
        load.start()

    barrier = pltpu.get_barrier_semaphore()
    ends = [targets(u, tiles, pair, chunks) for u in range(tiles)]
    greeted = 0
    if plan:
        for u in range(tiles):
            greeted = greeted + (t == u).astype(jnp.int32) * len(ends[u])

            @pl.when(t == u)
            def _():
                for v in range(tiles):
                    if u in ends[v]:
                        pl.semaphore_signal(barrier, inc=1, device_id={"tile": v}, device_id_type=pl.DeviceIdType.MESH)
    else:
        near = sorted({pair * d for d in range(1, depth)} | {1})
        for step in [sign * d for d in near for sign in (-1, 1)]:
            there = jnp.logical_and(t + step >= 0, t + step < tiles)
            greeted = greeted + there.astype(jnp.int32)

            @pl.when(there)
            def _():
                pl.semaphore_signal(barrier, inc=1, device_id={"tile": t + step}, device_id_type=pl.DeviceIdType.MESH)

    for d in range(1, members):
        pl.semaphore_signal(
            barrier, inc=1, device_id={"member": (m + d) % members}, device_id_type=pl.DeviceIdType.MESH
        )

    for load in loads[2:6] + moves + loads[6:]:
        load.start()
    for load in loads[:2]:
        load.wait()
    own = pl.multiple_of(t * rows, rows)
    n_hi, n_lo = split(noise[...])
    first = dot(jnp.concatenate([n_hi, n_lo], axis=0), txt[0])
    xg[pl.ds(own, rows), :] = (first[:rows] + first[rows:] + dot(n_hi, txt[1])).astype(BF16)
    pl.semaphore_wait(barrier, greeted + members - 1)

    def part(block, c):
        return xg.at[pl.ds(pl.multiple_of(block * rows + c * size, size), size), :]

    def along(up, d, c):
        mine = part(t, c)
        return pltpu.make_async_remote_copy(
            src_ref=mine, dst_ref=mine, send_sem=send_sem.at[up, d, c], recv_sem=recv_sem.at[t, c],
            device_id={"tile": t + pair * (d if up else -d)}, device_id_type=pl.DeviceIdType.MESH,
        )

    def across(zb, c):
        block = part(zb * pair + x, c)
        return pltpu.make_async_remote_copy(
            src_ref=block, dst_ref=block, send_sem=cross_sem.at[zb, c], recv_sem=recv_sem.at[zb * pair + x, c],
            device_id={"tile": z * pair + 1 - x}, device_id_type=pl.DeviceIdType.MESH,
        )

    def arrival(block, c):
        pltpu.make_async_copy(part(block, c), part(block, c), recv_sem.at[block, c]).wait()

    def both_ways(d, act):
        @pl.when(z + d < depth)
        def _():
            act(1)

        @pl.when(z - d >= 0)
        def _():
            act(0)

    def column(other):
        return 1 - x if other else x

    def message(number, block_z, block_other, c, end_z, end_other):
        block = block_z * pair + column(block_other)
        mine = part(block, c)
        return pltpu.make_async_remote_copy(
            src_ref=mine, dst_ref=mine, send_sem=plan_sem.at[0], recv_sem=plan_sem.at[number],
            device_id={"tile": end_z * pair + column(end_other)}, device_id_type=pl.DeviceIdType.MESH,
        )

    def slot(end_z, block_z, block_other, c):
        passed = [relay[:3] for relay in PLAN[end_z][1]]
        key = (block_z, block_other, c)
        return 2 + passed.index(key) if key in passed else 1

    def landed(number, count):
        bulk = spec.at[pl.ds(0, count * size // 2), :]
        pltpu.make_async_copy(bulk, bulk, plan_sem.at[number]).wait()

    def at_level(act):
        for k in range(depth):
            pl.when(z == k)(functools.partial(act, k, *PLAN[k]))

    def first_sends(k, first, relays):
        for c, a, b in first:
            message(slot(a, k, b, c), k, 0, c, a, b).start()

    def pass_on(k, first, relays):
        for i, (block_z, block_other, c, goals) in enumerate(relays):
            landed(2 + i, 1)
            for a, b in goals:
                message(slot(a, block_z, block_other ^ b, c), block_z, block_other, c, a, b).start()

    def last_arrivals(k, first, relays):
        landed(1, (tiles - 1) * chunks - len(relays))

    def sends_done(k, first, relays):
        landed(0, len(first) + sum(len(relay[3]) for relay in relays))

    if plan:
        at_level(first_sends)
    else:
        for c in range(chunks):
            if pair > 1:
                across(z, c).start()
            for d in range(depth - 1, 0, -1):
                both_ways(d, lambda up: along(up, d, c).start())

    def relay(s):
        def take(up, c):
            zb = z + s if up else z - s
            arrival(zb * pair + x, c)
            if pair > 1:
                across(zb, c).start()

        for c in range(chunks):
            both_ways(s, lambda up: take(up, c))

    for load in loads[2:6]:
        load.wait()
    coef = [coefficients(ac, scale, k, width) for k in range(LEVELS)]
    for g in range(rows // 16):
        span = pl.ds(16 * g, 16)
        total = jnp.zeros((16, width), F32)
        for k in range(LEVELS):
            total += coef[k][0] * obs[0, k, span, :].astype(F32) + coef[k][1] * obs[1, k, span, :].astype(F32)
        pad[pl.ds(PAD + 16 * g, 16), :] = total
    for i in range(rows // 8):
        for j in range(width // 128):
            mask[8 * i : 8 * i + 8, 128 * j : 128 * j + 128] = jnp.full((8, 128), rain[j, i].astype(F32), F32)

    after = pltpu.make_async_remote_copy(
        src_ref=pad.at[pl.ds(rows, PAD), :], dst_ref=pad.at[pl.ds(0, PAD), :],
        send_sem=halo_send.at[0], recv_sem=halo_recv.at[0],
        device_id={"tile": t + 1}, device_id_type=pl.DeviceIdType.MESH,
    )
    before = pltpu.make_async_remote_copy(
        src_ref=pad.at[pl.ds(PAD, PAD), :], dst_ref=pad.at[pl.ds(rows + PAD, PAD), :],
        send_sem=halo_send.at[1], recv_sem=halo_recv.at[1],
        device_id={"tile": t - 1}, device_id_type=pl.DeviceIdType.MESH,
    )

    @pl.when(t < tiles - 1)
    def _():
        after.start()

    @pl.when(t == tiles - 1)
    def _():
        pad[rows + PAD :, :] = jnp.zeros((PAD, width), F32)

    @pl.when(t > 0)
    def _():
        before.start()

    @pl.when(t == 0)
    def _():
        pad[:PAD, :] = jnp.zeros((PAD, width), F32)

    def shift_columns(start, count):
        lane = lax.broadcasted_iota(jnp.int32, (count, width), 1)
        value = pad[start : start + count, :]
        for dx in range(-HALO, HALO + 1):
            moved = pltpu.roll(value, dx % width, 1) if dx else value
            if dx > 0:
                moved = jnp.where(lane >= dx, moved, 0.0)
            if dx < 0:
                moved = jnp.where(lane < width + dx, moved, 0.0)
            shifted[dx + HALO, start : start + count, :] = moved

    def gather_rows(start, stop):
        for g in range(start, stop):
            span = pl.ds(8 * g, 8)
            code = shift[0, span, :] * (2 * HALO + 1) + shift[1, span, :]
            total = jnp.zeros((8, width), F32)
            for dy in range(-HALO, HALO + 1):
                for dx in range(-HALO, HALO + 1):
                    total = jnp.where(
                        code == dy * (2 * HALO + 1) + dx,
                        shifted[dx + HALO, 8 * g + PAD - dy : 8 * g + PAD - dy + 8, :],
                        total,
                    )
            steady[span, :] = total

    groups = rows // 8
    shift_columns(PAD, rows)
    both_moves.wait()
    gather_rows(1, groups - 1)

    if plan:
        at_level(pass_on)
    else:
        for s in range(1, depth):
            relay(s)

    @pl.when(t > 0)
    def _():
        after.wait_recv()

    @pl.when(t < tiles - 1)
    def _():
        before.wait_recv()

    shift_columns(0, PAD)
    shift_columns(rows + PAD, PAD)
    gather_rows(0, 1)
    gather_rows(max(groups - 1, 1), groups)
    for load in loads[6:]:
        load.wait()
    if plan:
        at_level(last_arrivals)
    elif pair > 1:
        for zb in range(depth):
            for c in range(chunks):
                arrival(zb * pair + 1 - x, c)

    spec[...] = dot(ty[...], xg[...])
    strip = 16
    lane = lax.broadcasted_iota(jnp.int32, (strip, hx), 1)
    lane_one = lax.broadcasted_iota(jnp.int32, (strip, 128), 1)
    sub = lax.broadcasted_iota(jnp.int32, (strip, hx), 0)

    def fold(value):
        return value[:8] + value[8:]

    def powers(i, sums):
        r = pl.multiple_of(i * strip, strip)
        top = pl.ds(r, strip)
        low = pl.ds(hy + r, strip)
        cc, cs = spec[top, :hx], spec[top, hx:]
        sc, ss = spec[low, :hx], spec[low, hx:]
        cc, cs, sc, ss = cc * cc, cs * cs, sc * sc, ss * ss
        inner = sub + r > 0
        sc = jnp.where(inner, sc, 0.0)
        ss = jnp.where(inner, ss, 0.0)
        right = cs + ss
        energy = cc + sc + jnp.where(lane > 0, right, 0.0)
        edge = jnp.where(lane_one == 0, right[:, :128], 0.0)
        out = []
        for k in range(LEVELS):
            w = band[k, top, :hx].astype(F32)
            e = band[k, top, hx:].astype(F32)
            out.append((sums[2 * k] + fold(w * w * energy)))
            out.append((sums[2 * k + 1] + fold(e * e * edge)))
        return tuple(out)

    sc, ss = spec[hy : hy + 8, :hx], spec[hy : hy + 8, hx:]
    sc, ss = sc * sc, ss * ss
    first_row = sub[:8] == 0
    bottom = jnp.where(first_row, sc + jnp.where(lane[:8] > 0, ss, 0.0), 0.0)
    corner = jnp.where(jnp.logical_and(first_row[:, :128], lane_one[:8] == 0), ss[:, :128], 0.0)
    sums = []
    for k in range(LEVELS):
        w = band[k, hy:, :hx].astype(F32)
        e = band[k, hy:, hx:].astype(F32)
        sums += [w * w * bottom, e * e * corner]
    sums = lax.fori_loop(0, hy // strip, powers, tuple(sums), unroll=2)
    levels = []
    for k in range(LEVELS):
        both = jnp.concatenate([sums[2 * k], sums[2 * k + 1]], axis=1)
        power = jnp.sum(jnp.sum(both, axis=0, keepdims=True), axis=1, keepdims=True) / float(height * width)
        levels.append(coef[k][2][:, :1] / jnp.sqrt(power + 1e-06))
    level = [jnp.broadcast_to(v, (1, hx + 128)) for v in levels]

    last = sum(level[k] * band[k, hy:, :].astype(F32) for k in range(LEVELS))[:1]

    def apply(i, carry):
        r = pl.multiple_of(i * strip, strip)
        top = pl.ds(r, strip)
        low = pl.ds(hy + r, strip)
        a = level[0] * band[0, top, :].astype(F32)
        for k in range(1, LEVELS):
            a += level[k] * band[k, top, :].astype(F32)

        def right_of(v):
            begin = jnp.where(lane_one == 0, v[:, hx:], v[:, :128])
            return jnp.concatenate([begin, v[:, 128:hx]], axis=1) if hx > 128 else begin

        gain[top, :hx] = (a[:, :hx] * spec[top, :hx]).astype(BF16)
        gain[top, hx:] = (right_of(a) * spec[top, hx:]).astype(BF16)
        wide = lax.broadcasted_iota(jnp.int32, (strip, hx + 128), 0) + r
        b = jnp.where(wide == 0, last, a)
        gain[low, :hx] = (b[:, :hx] * spec[low, :hx]).astype(BF16)
        gain[low, hx:] = (right_of(b) * spec[low, hx:]).astype(BF16)
        return carry

    lax.fori_loop(0, hy // strip, apply, 0, unroll=2)

    back = dot(jnp.concatenate([rows_t[0], rows_t[1]], axis=0), gain[...])
    b_hi, b_lo = split(back[:rows] + back[rows:])
    field = dot(jnp.concatenate([b_hi, b_lo], axis=0), tx[...])
    raw = (steady[...] + (field[:rows] + field[rows:])) * mask[...]
    mean[...] = raw
    fc[...] = raw.astype(BF16)

    sends = [
        pltpu.make_async_remote_copy(
            src_ref=fc, dst_ref=arrived.at[d - 1], send_sem=mem_send.at[0], recv_sem=mem_recv.at[0],
            device_id={"member": (m + d) % members}, device_id_type=pl.DeviceIdType.MESH,
        )
        for d in range(1, members)
    ]
    for send in sends:
        send.start()

    if plan:
        at_level(sends_done)
    else:
        for c in range(chunks):
            for d in range(1, depth):
                both_ways(d, lambda up: along(up, d, c).wait_send())
            if pair > 1:
                for zb in range(depth):
                    across(zb, c).wait_send()

    @pl.when(t < tiles - 1)
    def _():
        after.wait_send()

    @pl.when(t > 0)
    def _():
        before.wait_send()

    everyone = pltpu.make_async_copy(arrived, arrived, mem_recv.at[0])
    if members > 1:
        everyone.wait()
    total = mean[...]
    for d in range(1, members):
        total += arrived[d - 1].astype(F32)
    mean[...] = total * (1.0 / members)
    if members > 1:
        pltpu.make_async_copy(arrived, arrived, mem_send.at[0]).wait()


def shards(tables, tiles, members, noise, observed, row_shift, col_shift, rain_mask, autocorr, level_scale):
    _, rows, width = noise.shape
    height = rows * tiles
    pair = 2 if tiles % 2 == 0 else 1
    depth, chunks = tiles // pair, rows // chunk_of(rows)
    any_space = pl.BlockSpec(memory_space=pl.ANY)
    dma = pltpu.SemaphoreType.DMA
    plan = planned(tiles, pair, chunks)
    peers = max(members - 1, 1)
    fields = pl.pallas_call(
        functools.partial(kernel, tiles, pair, members),
        out_shape=(pltpu.VMEM((1, rows, width), BF16), pltpu.VMEM((rows, width), F32)),
        in_specs=[any_space] * 12,
        out_specs=(pl.BlockSpec(memory_space=pltpu.VMEM),) * 2,
        scratch_shapes=[
            pltpu.VMEM((rows, width), F32),
            pltpu.VMEM(observed.shape, BF16),
            pltpu.VMEM((2, rows, width), jnp.int32),
            pltpu.VMEM((height, height), BF16),
            pltpu.VMEM((width, width), BF16),
            pltpu.VMEM((2, width, width), BF16),
            pltpu.VMEM((2, rows, height), BF16),
            pltpu.VMEM(tables[-1].shape, BF16),
            pltpu.VMEM((height, width), BF16),
            pltpu.VMEM((rows + 2 * PAD, width), F32),
            pltpu.VMEM((2 * HALO + 1, rows + 2 * PAD, width), F32),
            pltpu.VMEM((rows, width), F32),
            pltpu.VMEM((rows, width), F32),
            pltpu.VMEM((height, width), F32),
            pltpu.VMEM((height, width), BF16),
            pltpu.VMEM((peers, rows, width), BF16),
            pltpu.SMEM(rain_mask.shape[::-1], jnp.int32),
            pltpu.SMEM(autocorr.shape, F32),
            pltpu.SMEM(level_scale.shape, F32),
            dma((11,)),
            *([dma((1,))] * 2 if plan else [dma((2, depth, chunks)), dma((depth, chunks))]),
            dma((plan_slots(),)) if plan else dma((1,)),
            dma((1,)) if plan else dma((tiles, chunks)),
            dma((2,)),
            dma((2,)),
            dma((1,)),
            dma((1,)),
        ],
        compiler_params=pltpu.CompilerParams(
            collective_id=0, has_side_effects=True, vmem_limit_bytes=67043328 - 4 * 64 * 1024
        ),
        name="nowcast",
    )(noise, observed, row_shift, col_shift, rain_mask.T, autocorr, level_scale, *tables)
    return pl.pallas_call(
        write_out,
        out_shape=(
            jax.ShapeDtypeStruct((1, rows, width), BF16),
            jax.ShapeDtypeStruct((rows, width), F32),
        ),
        in_specs=[pl.BlockSpec(memory_space=pltpu.VMEM)] * 2,
        out_specs=(any_space, any_space),
        scratch_shapes=[dma((2,))],
        compiler_params=pltpu.CompilerParams(vmem_limit_bytes=1024 * 1024),
        name="write_out",
    )(*fields)


def solution(mesh):
    tiles, members = mesh.shape["tile"], mesh.shape["member"]
    in_specs = (
        P("member", "tile", None),
        P(None, None, "tile", None),
        P("tile", None),
        P("tile", None),
        P("tile", None),
        P(),
        P(),
    )
    out_specs = (P("member", "tile", None), P("tile", None))

    def program(noise, observed, *rest):
        height, width = noise.shape[1:]

        def halves(table):
            high = table.astype(jnp.bfloat16)
            return high, (table - high.astype(np.float64)).astype(jnp.bfloat16)

        basis_y, basis_x = real_basis(height), real_basis(width)
        tables = (
            basis_y.astype(jnp.bfloat16),
            basis_x.astype(jnp.bfloat16),
            np.stack(halves(np.ascontiguousarray(basis_x.T))),
            np.stack(halves(np.ascontiguousarray(basis_y.T))),
            band_table(height, width).astype(jnp.bfloat16),
        )
        body = functools.partial(shards, tables, tiles, members)
        return jax.shard_map(body, mesh=mesh, in_specs=in_specs, out_specs=out_specs, check_vma=False)(
            noise, observed, *rest
        )

    return program
```

```python
import functools
import math

import jax
import jax.numpy as jnp
import numpy as np
from jax import lax
from jax.experimental import pallas as pl
from jax.experimental.pallas import tpu as pltpu
from jax.sharding import PartitionSpec as P

LEVELS = 6
HALO = 4
PAD = 8
F32 = jnp.float32
BF16 = jnp.bfloat16
PLAN = (
    (
        ((1, 0, 1), (1, 1, 0), (0, 0, 1), (0, 1, 0)),
        (
            (0, 1, 1, ((1, 0),)),
            (2, 0, 1, ((0, 1), (1, 0))),
            (2, 0, 0, ((0, 1), (1, 0))),
            (3, 0, 0, ((0, 1),)),
        ),
    ),
    (
        ((1, 3, 0), (1, 2, 0), (0, 2, 0), (0, 1, 1), (1, 0, 0), (1, 1, 1), (0, 0, 0)),
        (
            (0, 0, 1, ((3, 0),)),
            (0, 0, 0, ((1, 1), (3, 0))),
            (1, 1, 0, ((3, 0), (0, 0))),
            (1, 1, 1, ((0, 0), (3, 0))),
            (0, 1, 1, ((2, 0),)),
            (3, 0, 0, ((2, 0), (1, 1))),
            (0, 1, 0, ((2, 0),)),
        ),
    ),
    (
        ((1, 0, 0), (1, 2, 1), (0, 2, 1), (1, 3, 0), (0, 0, 0), (0, 3, 0)),
        (
            (2, 1, 1, ((1, 0),)),
            (2, 1, 0, ((1, 0),)),
            (3, 1, 1, ((0, 0), (3, 0), (1, 0))),
            (1, 0, 0, ((2, 1), (3, 0))),
            (3, 0, 1, ((1, 0),)),
        ),
    ),
    (
        ((0, 0, 0), (0, 3, 1), (1, 2, 1), (0, 1, 0), (1, 0, 0), (1, 2, 0)),
        (
            (2, 0, 1, ((3, 1),)),
            (3, 1, 0, ((2, 0),)),
            (2, 0, 0, ((3, 1),)),
            (1, 0, 1, ((2, 1),)),
            (0, 0, 1, ((2, 0), (3, 1))),
            (0, 0, 0, ((3, 1), (2, 0))),
        ),
    ),
)


def real_basis(length):
    half = length // 2
    positions = np.arange(length)
    angles = 2.0 * math.pi * (np.outer(np.arange(half), positions) % length) / length
    cosines = np.cos(angles) * math.sqrt(2.0 / length)
    sines = np.sin(angles) * math.sqrt(2.0 / length)
    cosines[0] = 1.0 / math.sqrt(length)
    sines[0] = (1.0 - 2.0 * (positions % 2)) / math.sqrt(length)
    return np.concatenate([cosines, sines], axis=0)


def band_table(height, width):
    freq_y = np.arange(height // 2 + PAD)[:, None] / height
    freq_x = np.arange(width // 2 + 128)[None, :] / width
    longest = max(height, width)
    log_radius = np.log(longest * np.sqrt(freq_y * freq_y + freq_x * freq_x) + 1.0)
    spacing = math.log(longest / 2.0) / (LEVELS - 1)
    offsets = log_radius[None] - spacing * np.arange(LEVELS)[:, None, None]
    bumps = np.exp(-(offsets * offsets) / (2.0 * (0.6 * spacing) ** 2))
    return bumps / np.sum(bumps, axis=0, keepdims=True)


def chunk_of(rows):
    return rows // 2 if rows % 32 == 0 else rows


def split(value):
    high = value.astype(BF16)
    return high, (value - high.astype(F32)).astype(BF16)


def planned(tiles, pair, chunks):
    chunk_count = 1 + max(send[0] for first, _ in PLAN for send in first)
    return pair == 2 and tiles == 2 * len(PLAN) and chunks == chunk_count


def plan_slots():
    return 2 + max(len(relays) for _, relays in PLAN)


def targets(t, tiles, pair, chunks):
    near = {u for u in (t - 1, t + 1) if 0 <= u < tiles}
    z, x = divmod(t, pair)
    if planned(tiles, pair, chunks):
        first, relays = PLAN[z]
        ends = {(a, b) for _, a, b in first} | {end for relay in relays for end in relay[3]}
        return near | {a * pair + (x ^ b) for a, b in ends}
    return near | {u * pair + x for u in range(tiles // pair) if u != z} | ({z * pair + 1 - x} if pair > 1 else set())


def dot(a, b):
    return jnp.dot(a, b, preferred_element_type=F32)


def coefficients(ac, scale, k, width):
    g1 = jnp.full((1, width), ac[0, k], F32)
    g2 = jnp.full((1, width), ac[1, k], F32)
    s = jnp.full((1, width), scale[k], F32)
    den = 1.0 - g1 * g1
    one = g1 * (1.0 - g2) / den
    two = (g2 - g1 * g1) / den
    innovation = jnp.sqrt(1.0 - one * g1 - two * g2)
    return s * one, s * two, s * innovation


def write_out(fc, mean, fc_hbm, mean_hbm, sem):
    copies = [pltpu.make_async_copy(a, b, sem.at[i]) for i, (a, b) in enumerate([(fc, fc_hbm), (mean, mean_hbm)])]
    for copy in copies:
        copy.start()
    for copy in copies:
        copy.wait()


def kernel(
    tiles, pair, members,
    noise_hbm, obs_hbm, row_hbm, col_hbm, rain_hbm, ac_hbm, scale_hbm, ty_hbm, tx_hbm, txt_hbm, tyt_hbm, band_hbm,
    fc_out, mean,
    noise, obs, shift, ty, tx, txt, rows_t, band,
    xg, pad, shifted, steady, mask, spec, gain, bands, squares, arrived, rain, ac, scale,
    load_sem, send_sem, cross_sem, plan_sem, recv_sem, halo_send, halo_recv, mem_send, mem_recv,
):
    fc = fc_out.at[0]
    rows, width = noise.shape
    height = rows * tiles
    hy, hx = height // 2, width // 2
    depth = tiles // pair
    size = chunk_of(rows)
    chunks = rows // size
    plan = planned(tiles, pair, chunks)
    t = lax.axis_index("tile")
    m = lax.axis_index("member")
    z = t // pair
    x = t % pair

    sources = [
        (noise_hbm.at[0], noise), (txt_hbm, txt),
        (rain_hbm, rain), (ac_hbm, ac), (scale_hbm, scale), (obs_hbm, obs),
        (ty_hbm, ty), (band_hbm, band),
        (tyt_hbm.at[:, pl.ds(pl.multiple_of(t * rows, rows), rows), :], rows_t), (tx_hbm, tx),
    ]
    loads = [pltpu.make_async_copy(a, b, load_sem.at[i]) for i, (a, b) in enumerate(sources)]
    moves = [pltpu.make_async_copy(a, shift.at[i], load_sem.at[len(sources)]) for i, a in enumerate((row_hbm, col_hbm))]
    both_moves = pltpu.make_async_copy(shift, shift, load_sem.at[len(sources)])
    for load in loads[:2]:
        load.start()

    barrier = pltpu.get_barrier_semaphore()
    ends = [targets(u, tiles, pair, chunks) for u in range(tiles)]
    greeted = 0
    if plan:
        for u in range(tiles):
            greeted = greeted + (t == u).astype(jnp.int32) * len(ends[u])

            @pl.when(t == u)
            def _():
                for v in range(tiles):
                    if u in ends[v]:
                        pl.semaphore_signal(barrier, inc=1, device_id={"tile": v}, device_id_type=pl.DeviceIdType.MESH)
    else:
        near = sorted({pair * d for d in range(1, depth)} | {1})
        for step in [sign * d for d in near for sign in (-1, 1)]:
            there = jnp.logical_and(t + step >= 0, t + step < tiles)
            greeted = greeted + there.astype(jnp.int32)

            @pl.when(there)
            def _():
                pl.semaphore_signal(barrier, inc=1, device_id={"tile": t + step}, device_id_type=pl.DeviceIdType.MESH)

    for d in range(1, members):
        pl.semaphore_signal(
            barrier, inc=1, device_id={"member": (m + d) % members}, device_id_type=pl.DeviceIdType.MESH
        )

    for load in loads[2:6] + moves + loads[6:]:
        load.start()
    for load in loads[:2]:
        load.wait()
    own = pl.multiple_of(t * rows, rows)
    n_hi, n_lo = split(noise[...])
    first = dot(jnp.concatenate([n_hi, n_lo], axis=0), txt[0])
    xg[pl.ds(own, rows), :] = (first[:rows] + first[rows:] + dot(n_hi, txt[1])).astype(BF16)
    pl.semaphore_wait(barrier, greeted + members - 1)

    def part(block, c):
        return xg.at[pl.ds(pl.multiple_of(block * rows + c * size, size), size), :]

    def along(up, d, c):
        mine = part(t, c)
        return pltpu.make_async_remote_copy(
            src_ref=mine, dst_ref=mine, send_sem=send_sem.at[up, d, c], recv_sem=recv_sem.at[t, c],
            device_id={"tile": t + pair * (d if up else -d)}, device_id_type=pl.DeviceIdType.MESH,
        )

    def across(zb, c):
        block = part(zb * pair + x, c)
        return pltpu.make_async_remote_copy(
            src_ref=block, dst_ref=block, send_sem=cross_sem.at[zb, c], recv_sem=recv_sem.at[zb * pair + x, c],
            device_id={"tile": z * pair + 1 - x}, device_id_type=pl.DeviceIdType.MESH,
        )

    def arrival(block, c):
        pltpu.make_async_copy(part(block, c), part(block, c), recv_sem.at[block, c]).wait()

    def both_ways(d, act):
        @pl.when(z + d < depth)
        def _():
            act(1)

        @pl.when(z - d >= 0)
        def _():
            act(0)

    def column(other):
        return 1 - x if other else x

    def message(number, block_z, block_other, c, end_z, end_other):
        block = block_z * pair + column(block_other)
        mine = part(block, c)
        return pltpu.make_async_remote_copy(
            src_ref=mine, dst_ref=mine, send_sem=plan_sem.at[0], recv_sem=plan_sem.at[number],
            device_id={"tile": end_z * pair + column(end_other)}, device_id_type=pl.DeviceIdType.MESH,
        )

    def slot(end_z, block_z, block_other, c):
        passed = [relay[:3] for relay in PLAN[end_z][1]]
        key = (block_z, block_other, c)
        return 2 + passed.index(key) if key in passed else 1

    def landed(number, count):
        bulk = spec.at[pl.ds(0, count * size // 2), :]
        pltpu.make_async_copy(bulk, bulk, plan_sem.at[number]).wait()

    def at_level(act):
        for k in range(depth):
            pl.when(z == k)(functools.partial(act, k, *PLAN[k]))

    def first_sends(k, first, relays):
        for c, a, b in first:
            message(slot(a, k, b, c), k, 0, c, a, b).start()

    def pass_on(k, first, relays):
        for i, (block_z, block_other, c, goals) in enumerate(relays):
            landed(2 + i, 1)
            for a, b in goals:
                message(slot(a, block_z, block_other ^ b, c), block_z, block_other, c, a, b).start()

    def last_arrivals(k, first, relays):
        landed(1, (tiles - 1) * chunks - len(relays))

    def sends_done(k, first, relays):
        landed(0, len(first) + sum(len(relay[3]) for relay in relays))

    if plan:
        at_level(first_sends)
    else:
        for c in range(chunks):
            if pair > 1:
                across(z, c).start()
            for d in range(depth - 1, 0, -1):
                both_ways(d, lambda up: along(up, d, c).start())

    def relay(s):
        def take(up, c):
            zb = z + s if up else z - s
            arrival(zb * pair + x, c)
            if pair > 1:
                across(zb, c).start()

        for c in range(chunks):
            both_ways(s, lambda up: take(up, c))

    for load in loads[2:6]:
        load.wait()
    coef = [coefficients(ac, scale, k, width) for k in range(LEVELS)]
    for g in range(rows // 16):
        span = pl.ds(16 * g, 16)
        total = jnp.zeros((16, width), F32)
        for k in range(LEVELS):
            total += coef[k][0] * obs[0, k, span, :].astype(F32) + coef[k][1] * obs[1, k, span, :].astype(F32)
        pad[pl.ds(PAD + 16 * g, 16), :] = total
    for i in range(rows // 8):
        for j in range(width // 128):
            mask[8 * i : 8 * i + 8, 128 * j : 128 * j + 128] = jnp.full((8, 128), rain[j, i].astype(F32), F32)

    after = pltpu.make_async_remote_copy(
        src_ref=pad.at[pl.ds(rows, PAD), :], dst_ref=pad.at[pl.ds(0, PAD), :],
        send_sem=halo_send.at[0], recv_sem=halo_recv.at[0],
        device_id={"tile": t + 1}, device_id_type=pl.DeviceIdType.MESH,
    )
    before = pltpu.make_async_remote_copy(
        src_ref=pad.at[pl.ds(PAD, PAD), :], dst_ref=pad.at[pl.ds(rows + PAD, PAD), :],
        send_sem=halo_send.at[1], recv_sem=halo_recv.at[1],
        device_id={"tile": t - 1}, device_id_type=pl.DeviceIdType.MESH,
    )

    @pl.when(t < tiles - 1)
    def _():
        after.start()

    @pl.when(t == tiles - 1)
    def _():
        pad[rows + PAD :, :] = jnp.zeros((PAD, width), F32)

    @pl.when(t > 0)
    def _():
        before.start()

    @pl.when(t == 0)
    def _():
        pad[:PAD, :] = jnp.zeros((PAD, width), F32)

    def shift_columns(start, count):
        lane = lax.broadcasted_iota(jnp.int32, (count, width), 1)
        value = pad[start : start + count, :]
        for dx in range(-HALO, HALO + 1):
            moved = pltpu.roll(value, dx % width, 1) if dx else value
            if dx > 0:
                moved = jnp.where(lane >= dx, moved, 0.0)
            if dx < 0:
                moved = jnp.where(lane < width + dx, moved, 0.0)
            shifted[dx + HALO, start : start + count, :] = moved

    def gather_rows(start, stop):
        for g in range(start, stop):
            span = pl.ds(8 * g, 8)
            code = shift[0, span, :] * (2 * HALO + 1) + shift[1, span, :]
            total = jnp.zeros((8, width), F32)
            for dy in range(-HALO, HALO + 1):
                for dx in range(-HALO, HALO + 1):
                    total = jnp.where(
                        code == dy * (2 * HALO + 1) + dx,
                        shifted[dx + HALO, 8 * g + PAD - dy : 8 * g + PAD - dy + 8, :],
                        total,
                    )
            steady[span, :] = total

    groups = rows // 8
    shift_columns(PAD, rows)
    both_moves.wait()
    gather_rows(1, groups - 1)

    if plan:
        at_level(pass_on)
    else:
        for s in range(1, depth):
            relay(s)

    @pl.when(t > 0)
    def _():
        after.wait_recv()

    @pl.when(t < tiles - 1)
    def _():
        before.wait_recv()

    shift_columns(0, PAD)
    shift_columns(rows + PAD, PAD)
    gather_rows(0, 1)
    gather_rows(max(groups - 1, 1), groups)
    for load in loads[6:]:
        load.wait()

    def widen(i, carry):
        span = pl.ds(pl.multiple_of(i * 8, 8), 8)
        for k in range(LEVELS):
            value = band[k, span, :].astype(F32)
            bands[k, span, :] = value
            squares[k, span, :] = value * value
        return carry

    lax.fori_loop(0, hy // 8 + 1, widen, 0)
    if plan:
        at_level(last_arrivals)
    elif pair > 1:
        for zb in range(depth):
            for c in range(chunks):
                arrival(zb * pair + 1 - x, c)

    spec[...] = dot(ty[...], xg[...])
    strip = 16
    lane = lax.broadcasted_iota(jnp.int32, (strip, hx), 1)
    lane_one = lax.broadcasted_iota(jnp.int32, (strip, 128), 1)
    sub = lax.broadcasted_iota(jnp.int32, (strip, hx), 0)

    def fold(value):
        return value[:8] + value[8:]

    def powers(i, sums):
        r = pl.multiple_of(i * strip, strip)
        top = pl.ds(r, strip)
        low = pl.ds(hy + r, strip)
        cc, cs = spec[top, :hx], spec[top, hx:]
        sc, ss = spec[low, :hx], spec[low, hx:]
        cc, cs, sc, ss = cc * cc, cs * cs, sc * sc, ss * ss
        inner = sub + r > 0
        sc = jnp.where(inner, sc, 0.0)
        ss = jnp.where(inner, ss, 0.0)
        right = cs + ss
        energy = cc + sc + jnp.where(lane > 0, right, 0.0)
        edge = jnp.where(lane_one == 0, right[:, :128], 0.0)
        out = []
        for k in range(LEVELS):
            out.append((sums[2 * k] + fold(squares[k, top, :hx] * energy)))
            out.append((sums[2 * k + 1] + fold(squares[k, top, hx:] * edge)))
        return tuple(out)

    sc, ss = spec[hy : hy + 8, :hx], spec[hy : hy + 8, hx:]
    sc, ss = sc * sc, ss * ss
    first_row = sub[:8] == 0
    bottom = jnp.where(first_row, sc + jnp.where(lane[:8] > 0, ss, 0.0), 0.0)
    corner = jnp.where(jnp.logical_and(first_row[:, :128], lane_one[:8] == 0), ss[:, :128], 0.0)
    sums = []
    for k in range(LEVELS):
        sums += [squares[k, hy:, :hx] * bottom, squares[k, hy:, hx:] * corner]
    sums = lax.fori_loop(0, hy // strip, powers, tuple(sums), unroll=2)
    levels = []
    for k in range(LEVELS):
        both = jnp.concatenate([sums[2 * k], sums[2 * k + 1]], axis=1)
        power = jnp.sum(jnp.sum(both, axis=0, keepdims=True), axis=1, keepdims=True) / float(height * width)
        levels.append(coef[k][2][:, :1] / jnp.sqrt(power + 1e-06))
    level = [jnp.broadcast_to(v, (1, hx + 128)) for v in levels]

    last = sum(level[k] * bands[k, hy:, :] for k in range(LEVELS))[:1]

    def apply(i, carry):
        r = pl.multiple_of(i * strip, strip)
        top = pl.ds(r, strip)
        low = pl.ds(hy + r, strip)
        a = level[0] * bands[0, top, :]
        for k in range(1, LEVELS):
            a += level[k] * bands[k, top, :]

        def right_of(v):
            begin = jnp.where(lane_one == 0, v[:, hx:], v[:, :128])
            return jnp.concatenate([begin, v[:, 128:hx]], axis=1) if hx > 128 else begin

        gain[top, :hx] = (a[:, :hx] * spec[top, :hx]).astype(BF16)
        gain[top, hx:] = (right_of(a) * spec[top, hx:]).astype(BF16)
        wide = lax.broadcasted_iota(jnp.int32, (strip, hx + 128), 0) + r
        b = jnp.where(wide == 0, last, a)
        gain[low, :hx] = (b[:, :hx] * spec[low, :hx]).astype(BF16)
        gain[low, hx:] = (right_of(b) * spec[low, hx:]).astype(BF16)
        return carry

    lax.fori_loop(0, hy // strip, apply, 0, unroll=2)

    back = dot(jnp.concatenate([rows_t[0], rows_t[1]], axis=0), gain[...])
    b_hi, b_lo = split(back[:rows] + back[rows:])
    field = dot(jnp.concatenate([b_hi, b_lo], axis=0), tx[...])
    raw = (steady[...] + (field[:rows] + field[rows:])) * mask[...]
    mean[...] = raw
    fc[...] = raw.astype(BF16)

    sends = [
        pltpu.make_async_remote_copy(
            src_ref=fc, dst_ref=arrived.at[d - 1], send_sem=mem_send.at[0], recv_sem=mem_recv.at[0],
            device_id={"member": (m + d) % members}, device_id_type=pl.DeviceIdType.MESH,
        )
        for d in range(1, members)
    ]
    for send in sends:
        send.start()

    if plan:
        at_level(sends_done)
    else:
        for c in range(chunks):
            for d in range(1, depth):
                both_ways(d, lambda up: along(up, d, c).wait_send())
            if pair > 1:
                for zb in range(depth):
                    across(zb, c).wait_send()

    @pl.when(t < tiles - 1)
    def _():
        after.wait_send()

    @pl.when(t > 0)
    def _():
        before.wait_send()

    everyone = pltpu.make_async_copy(arrived, arrived, mem_recv.at[0])
    if members > 1:
        everyone.wait()
    total = mean[...]
    for d in range(1, members):
        total += arrived[d - 1].astype(F32)
    mean[...] = total * (1.0 / members)
    if members > 1:
        pltpu.make_async_copy(arrived, arrived, mem_send.at[0]).wait()


def shards(tables, tiles, members, noise, observed, row_shift, col_shift, rain_mask, autocorr, level_scale):
    _, rows, width = noise.shape
    height = rows * tiles
    pair = 2 if tiles % 2 == 0 else 1
    depth, chunks = tiles // pair, rows // chunk_of(rows)
    any_space = pl.BlockSpec(memory_space=pl.ANY)
    dma = pltpu.SemaphoreType.DMA
    plan = planned(tiles, pair, chunks)
    peers = max(members - 1, 1)
    fields = pl.pallas_call(
        functools.partial(kernel, tiles, pair, members),
        out_shape=(pltpu.VMEM((1, rows, width), BF16), pltpu.VMEM((rows, width), F32)),
        in_specs=[any_space] * 12,
        out_specs=(pl.BlockSpec(memory_space=pltpu.VMEM),) * 2,
        scratch_shapes=[
            pltpu.VMEM((rows, width), F32),
            pltpu.VMEM(observed.shape, BF16),
            pltpu.VMEM((2, rows, width), jnp.int32),
            pltpu.VMEM((height, height), BF16),
            pltpu.VMEM((width, width), BF16),
            pltpu.VMEM((2, width, width), BF16),
            pltpu.VMEM((2, rows, height), BF16),
            pltpu.VMEM(tables[-1].shape, BF16),
            pltpu.VMEM((height, width), BF16),
            pltpu.VMEM((rows + 2 * PAD, width), F32),
            pltpu.VMEM((2 * HALO + 1, rows + 2 * PAD, width), F32),
            pltpu.VMEM((rows, width), F32),
            pltpu.VMEM((rows, width), F32),
            pltpu.VMEM((height, width), F32),
            pltpu.VMEM((height, width), BF16),
            pltpu.VMEM(tables[-1].shape, F32),
            pltpu.VMEM(tables[-1].shape, F32),
            pltpu.VMEM((peers, rows, width), BF16),
            pltpu.SMEM(rain_mask.shape[::-1], jnp.int32),
            pltpu.SMEM(autocorr.shape, F32),
            pltpu.SMEM(level_scale.shape, F32),
            dma((11,)),
            *([dma((1,))] * 2 if plan else [dma((2, depth, chunks)), dma((depth, chunks))]),
            dma((plan_slots(),)) if plan else dma((1,)),
            dma((1,)) if plan else dma((tiles, chunks)),
            dma((2,)),
            dma((2,)),
            dma((1,)),
            dma((1,)),
        ],
        compiler_params=pltpu.CompilerParams(
            collective_id=0, has_side_effects=True, vmem_limit_bytes=67043328 - 4 * 64 * 1024
        ),
        name="nowcast",
    )(noise, observed, row_shift, col_shift, rain_mask.T, autocorr, level_scale, *tables)
    return pl.pallas_call(
        write_out,
        out_shape=(
            jax.ShapeDtypeStruct((1, rows, width), BF16),
            jax.ShapeDtypeStruct((rows, width), F32),
        ),
        in_specs=[pl.BlockSpec(memory_space=pltpu.VMEM)] * 2,
        out_specs=(any_space, any_space),
        scratch_shapes=[dma((2,))],
        compiler_params=pltpu.CompilerParams(vmem_limit_bytes=1024 * 1024),
        name="write_out",
    )(*fields)


def solution(mesh):
    tiles, members = mesh.shape["tile"], mesh.shape["member"]
    in_specs = (
        P("member", "tile", None),
        P(None, None, "tile", None),
        P("tile", None),
        P("tile", None),
        P("tile", None),
        P(),
        P(),
    )
    out_specs = (P("member", "tile", None), P("tile", None))

    def program(noise, observed, *rest):
        height, width = noise.shape[1:]

        def halves(table):
            high = table.astype(jnp.bfloat16)
            return high, (table - high.astype(np.float64)).astype(jnp.bfloat16)

        basis_y, basis_x = real_basis(height), real_basis(width)
        tables = (
            basis_y.astype(jnp.bfloat16),
            basis_x.astype(jnp.bfloat16),
            np.stack(halves(np.ascontiguousarray(basis_x.T))),
            np.stack(halves(np.ascontiguousarray(basis_y.T))),
            band_table(height, width).astype(jnp.bfloat16),
        )
        body = functools.partial(shards, tables, tiles, members)
        return jax.shard_map(body, mesh=mesh, in_specs=in_specs, out_specs=out_specs, check_vma=False)(
            noise, observed, *rest
        )

    return program
```

```python
import functools
import math

import jax
import jax.numpy as jnp
import numpy as np
from jax import lax
from jax.experimental import pallas as pl
from jax.experimental.pallas import tpu as pltpu
from jax.sharding import PartitionSpec as P

LEVELS = 6
HALO = 4
PAD = 8
F32 = jnp.float32
BF16 = jnp.bfloat16
PLAN = (
    (
        ((0, 1, 0), (1, 3, 0), (0, 3, 0), (1, 0, 1), (0, 0, 1), (1, 1, 0), (1, 1, 1)),
        (
            (2, 1, 1, ((0, 1), (1, 1))),
            (2, 1, 0, ((0, 1), (1, 1))),
            (3, 0, 1, ((0, 1), (1, 1))),
        ),
    ),
    (
        ((0, 2, 1), (1, 1, 1), (0, 1, 1), (0, 3, 0), (1, 3, 0), (1, 0, 0), (0, 0, 0)),
        (
            (1, 1, 1, ((0, 0), (2, 0))),
            (0, 0, 0, ((2, 1), (2, 0), (1, 1))),
            (1, 1, 0, ((0, 0),)),
            (0, 0, 1, ((2, 1), (2, 0))),
        ),
    ),
    (
        ((1, 2, 1), (0, 3, 0), (1, 0, 1), (0, 2, 1), (1, 3, 0), (0, 0, 1)),
        (
            (2, 1, 1, ((3, 0), (1, 0))),
            (2, 1, 0, ((1, 0),)),
            (3, 0, 1, ((2, 1), (1, 0))),
            (3, 0, 0, ((2, 1), (1, 0))),
        ),
    ),
    (
        ((1, 0, 0), (1, 2, 0), (1, 3, 1), (0, 0, 0), (0, 3, 1), (0, 2, 0)),
        (
            (2, 0, 0, ((3, 1),)),
            (3, 1, 0, ((0, 0), (1, 0))),
            (1, 0, 0, ((3, 1), (2, 0))),
            (1, 0, 1, ((2, 0), (3, 1))),
            (0, 0, 1, ((3, 1),)),
            (0, 0, 0, ((3, 1),)),
        ),
    ),
)


def real_basis(length):
    half = length // 2
    positions = np.arange(length)
    angles = 2.0 * math.pi * (np.outer(np.arange(half), positions) % length) / length
    cosines = np.cos(angles) * math.sqrt(2.0 / length)
    sines = np.sin(angles) * math.sqrt(2.0 / length)
    cosines[0] = 1.0 / math.sqrt(length)
    sines[0] = (1.0 - 2.0 * (positions % 2)) / math.sqrt(length)
    return np.concatenate([cosines, sines], axis=0)


def band_table(height, width):
    freq_y = np.arange(height // 2 + PAD)[:, None] / height
    freq_x = np.arange(width // 2 + 128)[None, :] / width
    longest = max(height, width)
    log_radius = np.log(longest * np.sqrt(freq_y * freq_y + freq_x * freq_x) + 1.0)
    spacing = math.log(longest / 2.0) / (LEVELS - 1)
    offsets = log_radius[None] - spacing * np.arange(LEVELS)[:, None, None]
    bumps = np.exp(-(offsets * offsets) / (2.0 * (0.6 * spacing) ** 2))
    return bumps / np.sum(bumps, axis=0, keepdims=True)


def chunk_of(rows):
    return rows // 2 if rows % 32 == 0 else rows


def split(value):
    high = value.astype(BF16)
    return high, (value - high.astype(F32)).astype(BF16)


def planned(tiles, pair, chunks):
    chunk_count = 1 + max(send[0] for first, _ in PLAN for send in first)
    return pair == 2 and tiles == 2 * len(PLAN) and chunks == chunk_count


def plan_slots():
    return 2 + max(len(relays) for _, relays in PLAN)


def targets(t, tiles, pair, chunks):
    near = {u for u in (t - 1, t + 1) if 0 <= u < tiles}
    z, x = divmod(t, pair)
    if planned(tiles, pair, chunks):
        first, relays = PLAN[z]
        ends = {(a, b) for _, a, b in first} | {end for relay in relays for end in relay[3]}
        return near | {a * pair + (x ^ b) for a, b in ends}
    return near | {u * pair + x for u in range(tiles // pair) if u != z} | ({z * pair + 1 - x} if pair > 1 else set())


def dot(a, b):
    return jnp.dot(a, b, preferred_element_type=F32)


def coefficients(ac, scale, k, width):
    g1 = jnp.full((1, width), ac[0, k], F32)
    g2 = jnp.full((1, width), ac[1, k], F32)
    s = jnp.full((1, width), scale[k], F32)
    den = 1.0 - g1 * g1
    one = g1 * (1.0 - g2) / den
    two = (g2 - g1 * g1) / den
    innovation = jnp.sqrt(1.0 - one * g1 - two * g2)
    return s * one, s * two, s * innovation


def write_out(fc, mean, fc_hbm, mean_hbm, sem):
    copies = [pltpu.make_async_copy(a, b, sem.at[i]) for i, (a, b) in enumerate([(fc, fc_hbm), (mean, mean_hbm)])]
    for copy in copies:
        copy.start()
    for copy in copies:
        copy.wait()


def kernel(
    tiles, pair, members,
    noise_hbm, obs_hbm, row_hbm, col_hbm, rain_hbm, ac_hbm, scale_hbm, ty_hbm, tx_hbm, txt_hbm, tyt_hbm, band_hbm,
    fc_out, mean,
    noise, obs, shift, ty, tx, txt, rows_t, band,
    xg, pad, shifted, steady, mask, spec, gain, bands, squares, arrived, rain, ac, scale,
    load_sem, send_sem, cross_sem, plan_sem, recv_sem, halo_send, halo_recv, mem_send, mem_recv,
):
    fc = fc_out.at[0]
    rows, width = noise.shape
    height = rows * tiles
    hy, hx = height // 2, width // 2
    depth = tiles // pair
    size = chunk_of(rows)
    chunks = rows // size
    plan = planned(tiles, pair, chunks)
    t = lax.axis_index("tile")
    m = lax.axis_index("member")
    z = t // pair
    x = t % pair

    sources = [
        (noise_hbm.at[0], noise), (txt_hbm, txt),
        (rain_hbm, rain), (ac_hbm, ac), (scale_hbm, scale), (obs_hbm, obs),
        (ty_hbm, ty), (band_hbm, band),
        (tyt_hbm.at[:, pl.ds(pl.multiple_of(t * rows, rows), rows), :], rows_t), (tx_hbm, tx),
    ]
    loads = [pltpu.make_async_copy(a, b, load_sem.at[i]) for i, (a, b) in enumerate(sources)]
    moves = [pltpu.make_async_copy(a, shift.at[i], load_sem.at[len(sources)]) for i, a in enumerate((row_hbm, col_hbm))]
    both_moves = pltpu.make_async_copy(shift, shift, load_sem.at[len(sources)])
    for load in loads[:2]:
        load.start()

    barrier = pltpu.get_barrier_semaphore()
    ends = [targets(u, tiles, pair, chunks) for u in range(tiles)]
    greeted = 0
    if plan:
        for u in range(tiles):
            greeted = greeted + (t == u).astype(jnp.int32) * len(ends[u])

            @pl.when(t == u)
            def _():
                for v in range(tiles):
                    if u in ends[v]:
                        pl.semaphore_signal(barrier, inc=1, device_id={"tile": v}, device_id_type=pl.DeviceIdType.MESH)
    else:
        near = sorted({pair * d for d in range(1, depth)} | {1})
        for step in [sign * d for d in near for sign in (-1, 1)]:
            there = jnp.logical_and(t + step >= 0, t + step < tiles)
            greeted = greeted + there.astype(jnp.int32)

            @pl.when(there)
            def _():
                pl.semaphore_signal(barrier, inc=1, device_id={"tile": t + step}, device_id_type=pl.DeviceIdType.MESH)

    for d in range(1, members):
        pl.semaphore_signal(
            barrier, inc=1, device_id={"member": (m + d) % members}, device_id_type=pl.DeviceIdType.MESH
        )

    for load in loads[2:6] + moves + loads[6:]:
        load.start()
    for load in loads[:2]:
        load.wait()
    own = pl.multiple_of(t * rows, rows)
    n_hi, n_lo = split(noise[...])
    first = dot(jnp.concatenate([n_hi, n_lo], axis=0), txt[0])
    xg[pl.ds(own, rows), :] = (first[:rows] + first[rows:] + dot(n_hi, txt[1])).astype(BF16)
    pl.semaphore_wait(barrier, greeted + members - 1)

    def part(block, c):
        return xg.at[pl.ds(pl.multiple_of(block * rows + c * size, size), size), :]

    def along(up, d, c):
        mine = part(t, c)
        return pltpu.make_async_remote_copy(
            src_ref=mine, dst_ref=mine, send_sem=send_sem.at[up, d, c], recv_sem=recv_sem.at[t, c],
            device_id={"tile": t + pair * (d if up else -d)}, device_id_type=pl.DeviceIdType.MESH,
        )

    def across(zb, c):
        block = part(zb * pair + x, c)
        return pltpu.make_async_remote_copy(
            src_ref=block, dst_ref=block, send_sem=cross_sem.at[zb, c], recv_sem=recv_sem.at[zb * pair + x, c],
            device_id={"tile": z * pair + 1 - x}, device_id_type=pl.DeviceIdType.MESH,
        )

    def arrival(block, c):
        pltpu.make_async_copy(part(block, c), part(block, c), recv_sem.at[block, c]).wait()

    def both_ways(d, act):
        @pl.when(z + d < depth)
        def _():
            act(1)

        @pl.when(z - d >= 0)
        def _():
            act(0)

    def column(other):
        return 1 - x if other else x

    def message(number, block_z, block_other, c, end_z, end_other):
        block = block_z * pair + column(block_other)
        mine = part(block, c)
        return pltpu.make_async_remote_copy(
            src_ref=mine, dst_ref=mine, send_sem=plan_sem.at[0], recv_sem=plan_sem.at[number],
            device_id={"tile": end_z * pair + column(end_other)}, device_id_type=pl.DeviceIdType.MESH,
        )

    def slot(end_z, block_z, block_other, c):
        passed = [relay[:3] for relay in PLAN[end_z][1]]
        key = (block_z, block_other, c)
        return 2 + passed.index(key) if key in passed else 1

    def landed(number, count):
        bulk = spec.at[pl.ds(0, count * size // 2), :]
        pltpu.make_async_copy(bulk, bulk, plan_sem.at[number]).wait()

    def at_level(act):
        for k in range(depth):
            pl.when(z == k)(functools.partial(act, k, *PLAN[k]))

    def first_sends(k, first, relays):
        for c, a, b in first:
            message(slot(a, k, b, c), k, 0, c, a, b).start()

    def pass_on(k, first, relays):
        for i, (block_z, block_other, c, goals) in enumerate(relays):
            landed(2 + i, 1)
            for a, b in goals:
                message(slot(a, block_z, block_other ^ b, c), block_z, block_other, c, a, b).start()

    def last_arrivals(k, first, relays):
        landed(1, (tiles - 1) * chunks - len(relays))

    def sends_done(k, first, relays):
        landed(0, len(first) + sum(len(relay[3]) for relay in relays))

    if plan:
        at_level(first_sends)
    else:
        for c in range(chunks):
            if pair > 1:
                across(z, c).start()
            for d in range(depth - 1, 0, -1):
                both_ways(d, lambda up: along(up, d, c).start())

    def relay(s):
        def take(up, c):
            zb = z + s if up else z - s
            arrival(zb * pair + x, c)
            if pair > 1:
                across(zb, c).start()

        for c in range(chunks):
            both_ways(s, lambda up: take(up, c))

    for load in loads[2:6]:
        load.wait()
    coef = [coefficients(ac, scale, k, width) for k in range(LEVELS)]
    for g in range(rows // 16):
        span = pl.ds(16 * g, 16)
        total = jnp.zeros((16, width), F32)
        for k in range(LEVELS):
            total += coef[k][0] * obs[0, k, span, :].astype(F32) + coef[k][1] * obs[1, k, span, :].astype(F32)
        pad[pl.ds(PAD + 16 * g, 16), :] = total
    for i in range(rows // 8):
        for j in range(width // 128):
            mask[8 * i : 8 * i + 8, 128 * j : 128 * j + 128] = jnp.full((8, 128), rain[j, i].astype(F32), F32)

    after = pltpu.make_async_remote_copy(
        src_ref=pad.at[pl.ds(rows, PAD), :], dst_ref=pad.at[pl.ds(0, PAD), :],
        send_sem=halo_send.at[0], recv_sem=halo_recv.at[0],
        device_id={"tile": t + 1}, device_id_type=pl.DeviceIdType.MESH,
    )
    before = pltpu.make_async_remote_copy(
        src_ref=pad.at[pl.ds(PAD, PAD), :], dst_ref=pad.at[pl.ds(rows + PAD, PAD), :],
        send_sem=halo_send.at[1], recv_sem=halo_recv.at[1],
        device_id={"tile": t - 1}, device_id_type=pl.DeviceIdType.MESH,
    )

    @pl.when(t < tiles - 1)
    def _():
        after.start()

    @pl.when(t == tiles - 1)
    def _():
        pad[rows + PAD :, :] = jnp.zeros((PAD, width), F32)

    @pl.when(t > 0)
    def _():
        before.start()

    @pl.when(t == 0)
    def _():
        pad[:PAD, :] = jnp.zeros((PAD, width), F32)

    def shift_columns(start, count):
        lane = lax.broadcasted_iota(jnp.int32, (count, width), 1)
        value = pad[start : start + count, :]
        for dx in range(-HALO, HALO + 1):
            moved = pltpu.roll(value, dx % width, 1) if dx else value
            if dx > 0:
                moved = jnp.where(lane >= dx, moved, 0.0)
            if dx < 0:
                moved = jnp.where(lane < width + dx, moved, 0.0)
            shifted[dx + HALO, start : start + count, :] = moved

    def gather_rows(start, stop):
        for g in range(start, stop):
            span = pl.ds(8 * g, 8)
            code = shift[0, span, :] * (2 * HALO + 1) + shift[1, span, :]
            total = jnp.zeros((8, width), F32)
            for dy in range(-HALO, HALO + 1):
                for dx in range(-HALO, HALO + 1):
                    total = jnp.where(
                        code == dy * (2 * HALO + 1) + dx,
                        shifted[dx + HALO, 8 * g + PAD - dy : 8 * g + PAD - dy + 8, :],
                        total,
                    )
            steady[span, :] = total

    groups = rows // 8
    shift_columns(PAD, rows)
    both_moves.wait()
    gather_rows(1, groups - 1)

    if plan:
        at_level(pass_on)
    else:
        for s in range(1, depth):
            relay(s)

    @pl.when(t > 0)
    def _():
        after.wait_recv()

    @pl.when(t < tiles - 1)
    def _():
        before.wait_recv()

    shift_columns(0, PAD)
    shift_columns(rows + PAD, PAD)
    gather_rows(0, 1)
    gather_rows(max(groups - 1, 1), groups)
    for load in loads[6:]:
        load.wait()

    def widen(i, carry):
        span = pl.ds(pl.multiple_of(i * 8, 8), 8)
        for k in range(LEVELS):
            value = band[k, span, :].astype(F32)
            bands[k, span, :] = value
            squares[k, span, :] = value * value
        return carry

    lax.fori_loop(0, hy // 8 + 1, widen, 0)
    if plan:
        at_level(last_arrivals)
    elif pair > 1:
        for zb in range(depth):
            for c in range(chunks):
                arrival(zb * pair + 1 - x, c)

    spec[...] = dot(ty[...], xg[...])
    strip = 16
    lane = lax.broadcasted_iota(jnp.int32, (strip, hx), 1)
    lane_one = lax.broadcasted_iota(jnp.int32, (strip, 128), 1)
    sub = lax.broadcasted_iota(jnp.int32, (strip, hx), 0)

    def fold(value):
        return value[:8] + value[8:]

    def powers(i, sums):
        r = pl.multiple_of(i * strip, strip)
        top = pl.ds(r, strip)
        low = pl.ds(hy + r, strip)
        cc, cs = spec[top, :hx], spec[top, hx:]
        sc, ss = spec[low, :hx], spec[low, hx:]
        cc, cs, sc, ss = cc * cc, cs * cs, sc * sc, ss * ss
        inner = sub + r > 0
        sc = jnp.where(inner, sc, 0.0)
        ss = jnp.where(inner, ss, 0.0)
        right = cs + ss
        energy = cc + sc + jnp.where(lane > 0, right, 0.0)
        edge = jnp.where(lane_one == 0, right[:, :128], 0.0)
        out = []
        for k in range(LEVELS):
            out.append((sums[2 * k] + fold(squares[k, top, :hx] * energy)))
            out.append((sums[2 * k + 1] + fold(squares[k, top, hx:] * edge)))
        return tuple(out)

    sc, ss = spec[hy : hy + 8, :hx], spec[hy : hy + 8, hx:]
    sc, ss = sc * sc, ss * ss
    first_row = sub[:8] == 0
    bottom = jnp.where(first_row, sc + jnp.where(lane[:8] > 0, ss, 0.0), 0.0)
    corner = jnp.where(jnp.logical_and(first_row[:, :128], lane_one[:8] == 0), ss[:, :128], 0.0)
    sums = []
    for k in range(LEVELS):
        sums += [squares[k, hy:, :hx] * bottom, squares[k, hy:, hx:] * corner]
    sums = lax.fori_loop(0, hy // strip, powers, tuple(sums), unroll=2)
    levels = []
    for k in range(LEVELS):
        both = jnp.concatenate([sums[2 * k], sums[2 * k + 1]], axis=1)
        power = jnp.sum(jnp.sum(both, axis=0, keepdims=True), axis=1, keepdims=True) / float(height * width)
        levels.append(coef[k][2][:, :1] / jnp.sqrt(power + 1e-06))
    level = [jnp.broadcast_to(v, (1, hx + 128)) for v in levels]

    last = sum(level[k] * bands[k, hy:, :] for k in range(LEVELS))[:1]

    def apply(i, carry):
        r = pl.multiple_of(i * strip, strip)
        top = pl.ds(r, strip)
        low = pl.ds(hy + r, strip)
        a = level[0] * bands[0, top, :]
        for k in range(1, LEVELS):
            a += level[k] * bands[k, top, :]

        def right_of(v):
            begin = jnp.where(lane_one == 0, v[:, hx:], v[:, :128])
            return jnp.concatenate([begin, v[:, 128:hx]], axis=1) if hx > 128 else begin

        gain[top, :hx] = (a[:, :hx] * spec[top, :hx]).astype(BF16)
        gain[top, hx:] = (right_of(a) * spec[top, hx:]).astype(BF16)
        wide = lax.broadcasted_iota(jnp.int32, (strip, hx + 128), 0) + r
        b = jnp.where(wide == 0, last, a)
        gain[low, :hx] = (b[:, :hx] * spec[low, :hx]).astype(BF16)
        gain[low, hx:] = (right_of(b) * spec[low, hx:]).astype(BF16)
        return carry

    lax.fori_loop(0, hy // strip, apply, 0, unroll=2)

    back = dot(jnp.concatenate([rows_t[0], rows_t[1]], axis=0), gain[...])
    b_hi, b_lo = split(back[:rows] + back[rows:])
    field = dot(jnp.concatenate([b_hi, b_lo], axis=0), tx[...])
    raw = (steady[...] + (field[:rows] + field[rows:])) * mask[...]
    mean[...] = raw
    fc[...] = raw.astype(BF16)

    sends = [
        pltpu.make_async_remote_copy(
            src_ref=fc, dst_ref=arrived.at[d - 1], send_sem=mem_send.at[0], recv_sem=mem_recv.at[0],
            device_id={"member": (m + d) % members}, device_id_type=pl.DeviceIdType.MESH,
        )
        for d in range(1, members)
    ]
    for send in sends:
        send.start()

    if plan:
        at_level(sends_done)
    else:
        for c in range(chunks):
            for d in range(1, depth):
                both_ways(d, lambda up: along(up, d, c).wait_send())
            if pair > 1:
                for zb in range(depth):
                    across(zb, c).wait_send()

    @pl.when(t < tiles - 1)
    def _():
        after.wait_send()

    @pl.when(t > 0)
    def _():
        before.wait_send()

    everyone = pltpu.make_async_copy(arrived, arrived, mem_recv.at[0])
    if members > 1:
        everyone.wait()
    total = mean[...]
    for d in range(1, members):
        total += arrived[d - 1].astype(F32)
    mean[...] = total * (1.0 / members)
    if members > 1:
        pltpu.make_async_copy(arrived, arrived, mem_send.at[0]).wait()


def shards(tables, tiles, members, noise, observed, row_shift, col_shift, rain_mask, autocorr, level_scale):
    _, rows, width = noise.shape
    height = rows * tiles
    pair = 2 if tiles % 2 == 0 else 1
    depth, chunks = tiles // pair, rows // chunk_of(rows)
    any_space = pl.BlockSpec(memory_space=pl.ANY)
    dma = pltpu.SemaphoreType.DMA
    plan = planned(tiles, pair, chunks)
    peers = max(members - 1, 1)
    fields = pl.pallas_call(
        functools.partial(kernel, tiles, pair, members),
        out_shape=(pltpu.VMEM((1, rows, width), BF16), pltpu.VMEM((rows, width), F32)),
        in_specs=[any_space] * 12,
        out_specs=(pl.BlockSpec(memory_space=pltpu.VMEM),) * 2,
        scratch_shapes=[
            pltpu.VMEM((rows, width), F32),
            pltpu.VMEM(observed.shape, BF16),
            pltpu.VMEM((2, rows, width), jnp.int32),
            pltpu.VMEM((height, height), BF16),
            pltpu.VMEM((width, width), BF16),
            pltpu.VMEM((2, width, width), BF16),
            pltpu.VMEM((2, rows, height), BF16),
            pltpu.VMEM(tables[-1].shape, BF16),
            pltpu.VMEM((height, width), BF16),
            pltpu.VMEM((rows + 2 * PAD, width), F32),
            pltpu.VMEM((2 * HALO + 1, rows + 2 * PAD, width), F32),
            pltpu.VMEM((rows, width), F32),
            pltpu.VMEM((rows, width), F32),
            pltpu.VMEM((height, width), F32),
            pltpu.VMEM((height, width), BF16),
            pltpu.VMEM(tables[-1].shape, F32),
            pltpu.VMEM(tables[-1].shape, F32),
            pltpu.VMEM((peers, rows, width), BF16),
            pltpu.SMEM(rain_mask.shape[::-1], jnp.int32),
            pltpu.SMEM(autocorr.shape, F32),
            pltpu.SMEM(level_scale.shape, F32),
            dma((11,)),
            *([dma((1,))] * 2 if plan else [dma((2, depth, chunks)), dma((depth, chunks))]),
            dma((plan_slots(),)) if plan else dma((1,)),
            dma((1,)) if plan else dma((tiles, chunks)),
            dma((2,)),
            dma((2,)),
            dma((1,)),
            dma((1,)),
        ],
        compiler_params=pltpu.CompilerParams(
            collective_id=0, has_side_effects=True, vmem_limit_bytes=67043328 - 4 * 64 * 1024
        ),
        name="nowcast",
    )(noise, observed, row_shift, col_shift, rain_mask.T, autocorr, level_scale, *tables)
    return pl.pallas_call(
        write_out,
        out_shape=(
            jax.ShapeDtypeStruct((1, rows, width), BF16),
            jax.ShapeDtypeStruct((rows, width), F32),
        ),
        in_specs=[pl.BlockSpec(memory_space=pltpu.VMEM)] * 2,
        out_specs=(any_space, any_space),
        scratch_shapes=[dma((2,))],
        compiler_params=pltpu.CompilerParams(vmem_limit_bytes=1024 * 1024),
        name="write_out",
    )(*fields)


def solution(mesh):
    tiles, members = mesh.shape["tile"], mesh.shape["member"]
    in_specs = (
        P("member", "tile", None),
        P(None, None, "tile", None),
        P("tile", None),
        P("tile", None),
        P("tile", None),
        P(),
        P(),
    )
    out_specs = (P("member", "tile", None), P("tile", None))

    def program(noise, observed, *rest):
        height, width = noise.shape[1:]

        def halves(table):
            high = table.astype(jnp.bfloat16)
            return high, (table - high.astype(np.float64)).astype(jnp.bfloat16)

        basis_y, basis_x = real_basis(height), real_basis(width)
        tables = (
            basis_y.astype(jnp.bfloat16),
            basis_x.astype(jnp.bfloat16),
            np.stack(halves(np.ascontiguousarray(basis_x.T))),
            np.stack(halves(np.ascontiguousarray(basis_y.T))),
            band_table(height, width).astype(jnp.bfloat16),
        )
        body = functools.partial(shards, tables, tiles, members)
        return jax.shard_map(body, mesh=mesh, in_specs=in_specs, out_specs=out_specs, check_vma=False)(
            noise, observed, *rest
        )

    return program
```
